128 devices in a mesh: gx: 16 (over z_lo, x, core), gz: 8 (over y, z_hi).
Axes of the slice: x: 4, y: 4, z: 4 (z_hi: 2, z_lo: 2; z = z_hi * 2 + z_lo), core: 2. Of those that a mesh axis runs over, the one named last changes fastest.
Arguments:
- elevation: float32 [2048, 2048], P(('gx', 'gz')), may hold values from -2 to 2
- potential: float32 [2048, 2048], P(('gx', 'gz')), may hold values from -6 to 6
- tracer: float32 [2048, 64, 256], P('gx', 'gz'), may hold values from -6 to 6
- wind_speed: float32 [2048, 64, 256], P('gx', 'gz'), may hold values from -4 to 4
Outputs:
- new_elevation: float32 [2048, 2048], P(('gx', 'gz'))
- new_tracer: float32 [2048, 64, 256], P('gx', 'gz')
The draws below stay inside these ranges and needn't reach their ends.
All inputs are finite; a program needn't handle non-finite values.
Results may differ from the reference program's by a relative error of at most 0.00019.
Values sent between devices are 32-bit elements; how exact they have to be, the bound alone decides.
No kernel may reach another device: no remote copies, remote signals or barrier semaphores. Data moves between devices by JAX's collectives and lax.ppermute only.
A program may use at most 128 MiB of HBM per device.

```python
import jax
import jax.numpy as jnp

NS = 2048
YA = 256
LEV = 64


def steps_of(stream_key, extent, shards, smallest, largest):
    loudness = 1.0
    for axis_at, shards_of in shards:
        heights = jax.random.uniform(jax.random.fold_in(jax.random.fold_in(stream_key, 6), axis_at), (shards_of,), jnp.float32, smallest / len(shards), largest / len(shards))
        loudness = loudness * jnp.repeat(jnp.exp(heights), extent[axis_at] // shards_of).reshape((-1,) + (1,) * (len(extent) - 1 - axis_at))
    return loudness


def normal_values(key, extent, spread, reach, split=(), held_as=jnp.bfloat16):
    factor_of = steps_of(key, extent, split, -0.22, 0.18) if split else 1.0
    entries = jax.random.normal(key, extent, jnp.float32) * spread * factor_of
    return jnp.minimum(jnp.maximum(entries, -reach), reach).astype(held_as)


def setup_inputs(seed: int = 0) -> dict:
    keys = jax.random.split(jax.random.key(seed), 5)
    elevation = normal_values(keys[0], (NS, NS), 0.15, 2.0, ((0, 128),), jnp.float32)
    potential = normal_values(keys[1], (NS, NS), 1.0, 6.0, ((0, 128),), jnp.float32)
    tracer = normal_values(keys[2], (NS, LEV, YA), 1.0, 6.0, ((0, 16), (1, 8)), jnp.float32)
    wind_speed = normal_values(keys[3], (NS, LEV, YA), 1.0, 4.0, ((0, 16), (1, 8)), jnp.float32)
    return dict(elevation=elevation, potential=potential, tracer=tracer, wind_speed=wind_speed)


TWO_PI = 6.283185307179586
DT_WAVE = 0.05
COLUMN_DEPTH = 32.0
DT_AIR = 0.1
NU_AIR = 0.2

def wave_numbers(length):
    positions = jnp.arange(length, dtype=jnp.int32)
    signed = jnp.where(positions < length // 2, positions, positions - length).astype(jnp.float32) * (TWO_PI / length)
    odd_wave = jnp.where(positions == length // 2, 0.0, signed)
    return (signed, odd_wave)

def to_field(spectrum):
    return jnp.real(jnp.fft.ifft2(spectrum)).astype(jnp.float32)

def mirror_levels(field):
    lower_level = jnp.concatenate([field[:, :1], field[:, :-1]], 1)
    upper_level = jnp.concatenate([field[:, 1:], field[:, -1:]], 1)
    return (lower_level, upper_level)

def reference(elevation, potential, tracer, wind_speed):
    signed, odd_wave = wave_numbers(NS)
    magnitude = jnp.sqrt(signed[:, None] * signed[:, None] + signed[None, :] * signed[None, :])
    squared = magnitude * magnitude
    magnitude_cube = squared * magnitude
    along_x = 1j * odd_wave[:, None]
    along_y = 1j * odd_wave[None, :]
    eta_spec = jnp.fft.fft2(elevation)
    phi_spec = jnp.fft.fft2(potential)
    first_once = to_field(magnitude * phi_spec)
    first_twice = to_field(squared * phi_spec)
    first_thrice = to_field(magnitude_cube * phi_spec)
    slope_x = to_field(along_x * eta_spec)
    slope_y = to_field(along_y * eta_spec)
    speed_x = to_field(along_x * phi_spec)
    speed_y = to_field(along_y * phi_spec)
    second_field = -elevation * first_once
    second_spec = jnp.fft.fft2(second_field)
    second_once = to_field(magnitude * second_spec)
    second_twice = to_field(squared * second_spec)
    third_field = -elevation * second_once - 0.5 * elevation * elevation * first_twice
    third_once = to_field(magnitude * jnp.fft.fft2(third_field))
    vertical = first_once + elevation * first_twice + 0.5 * elevation * elevation * first_thrice + second_once + elevation * second_twice + third_once
    tendency = -(slope_x * speed_x + slope_y * speed_y) + (1.0 + slope_x * slope_x + slope_y * slope_y) * vertical
    new_elevation = elevation + DT_WAVE * tendency
    new_slope = to_field(along_x * jnp.fft.fft2(new_elevation))
    old_rows = elevation[:, :YA]
    new_rows = new_elevation[:, :YA]
    slope_rows = new_slope[:, :YA]
    eastern = jnp.roll(tracer, -1, 0)
    western = jnp.roll(tracer, 1, 0)
    northern = jnp.concatenate([tracer[:, :, 1:], tracer[:, :, -1:]], 2)
    southern = jnp.concatenate([tracer[:, :, :1], tracer[:, :, :-1]], 2)
    moved_tracer = tracer + DT_AIR * (-wind_speed * (eastern - western) * 0.5 + NU_AIR * (eastern + western + northern + southern - 4.0 * tracer))
    sigma_level = (jnp.arange(LEV, dtype=jnp.int32).astype(jnp.float32) + 0.5) / LEV
    lift_factor = (1.0 - sigma_level)[None, :, None]
    level_shift = ((new_rows - old_rows) / (COLUMN_DEPTH - old_rows))[:, None, :] * lift_factor * LEV
    lower_level, upper_level = mirror_levels(moved_tracer)
    remapped = moved_tracer + 0.5 * level_shift * (upper_level - lower_level) + 0.5 * level_shift * level_shift * (upper_level - 2.0 * moved_tracer + lower_level)
    lower_level, upper_level = mirror_levels(remapped)
    column_depth = (COLUMN_DEPTH - new_rows)[:, None, :]
    advection = wind_speed * lift_factor * slope_rows[:, None, :] / column_depth * (upper_level - lower_level) * (0.5 * LEV)
    spread_term = NU_AIR * (upper_level - 2.0 * remapped + lower_level) * (LEV * LEV) / (column_depth * column_depth)
    new_tracer = remapped + DT_AIR * (advection + spread_term)
    return (new_elevation, new_tracer)
```

```python
import functools

import jax
import jax.numpy as jnp
import ml_dtypes
import numpy as np
from jax import lax
from jax.experimental import pallas as pl
from jax.experimental.pallas import tpu as pltpu
from jax.sharding import PartitionSpec as P

NS = 2048
DT_WAVE = 0.05
COLUMN_DEPTH = 32.0
DT_AIR = 0.1
NU_AIR = 0.2
TWO_PI = 6.283185307179586
WAVE_UNIT = TWO_PI / NS
BOTH = ("gx", "gz")
F32 = jnp.float32
BF16 = jnp.bfloat16


def halves(matrix):
    exact = np.asarray(matrix, np.float64)
    lead = exact.astype(np.float32).astype(ml_dtypes.bfloat16)
    rest = (exact - lead.astype(np.float64)).astype(np.float32).astype(ml_dtypes.bfloat16)
    return np.stack([lead, rest])


@functools.cache
def tables():
    n128, n16 = np.arange(128), np.arange(16)
    eye16, eye8 = np.eye(16), np.eye(8)
    turn = 2 * np.pi * (np.outer(n128, n128) % 128) / 128
    c, s = np.cos(turn), np.sin(turn)
    far = np.block([[c, s], [-s, c]])
    edge = np.zeros((2, 128, 2, 128))
    edge_back = np.zeros((2, 128, 2, 128))
    sign = (-1.0) ** n128
    for d in range(128):
        if d < 64:
            angle, part = 2 * np.pi * n128 * d / 128, 0
        else:
            angle, part = 2 * np.pi * n128 * (2 * (d - 64) + 1) / 256, 1
        edge[0, d, part] = np.cos(angle)
        edge[1, d, part] = -np.sin(angle) if d else sign
        weight = 2.0 if d else 1.0
        edge_back[part, :, 0, d] = weight * np.cos(angle)
        edge_back[part, :, 1, d] = -weight * np.sin(angle) if d else sign
    edge = edge.reshape(256, 256)
    edge_back = edge_back.reshape(256, 256)
    k8 = np.arange(8)
    angle = 2 * np.pi * np.outer(n16, k8) / 16
    near_re, near_im = np.cos(angle), -np.sin(angle)
    near_im[:, 0] = (-1.0) ** n16
    weight = np.where(k8 == 0, 1.0, 2.0)
    near = np.zeros((16, 16, 2, 8, 16))
    near_back = np.zeros((2, 8, 16, 16, 16))
    for part, table in enumerate((near_re, near_im)):
        near[:, :, part] = table[:, None, :, None] * eye16[None, :, None, :]
        near_back[part] = (table * weight).T[:, None, :, None] * eye16[None, :, None, :]
    near = near.reshape(256, 256)
    near_back = near_back.reshape(256, 256)
    angle = 2 * np.pi * np.outer(n16, n16) / 16
    cx, sx = np.kron(eye8, np.cos(angle)), np.kron(eye8, np.sin(angle))
    side = np.block([[cx, -sx], [sx, cx]])
    y_angle = 2 * np.pi * np.repeat(np.outer(n128, k8), 16, axis=1) / NS
    x_angle = 2 * np.pi * np.tile(np.outer(n128, n16), (1, 8)) / NS
    twist = lambda a: np.stack([np.cos(a), -np.sin(a)]).astype(np.float32)
    r = n128[None, :, None, None]
    x = 16 * n128[None, None, :, None] + n16.reshape(4, 1, 1, 4)
    n = r - x
    with np.errstate(divide="ignore", invalid="ignore"):
        slope = np.where(n % NS == 0, 0.0, (np.pi / NS) * (-1.0) ** (n % 2) / np.tan(np.pi * n / NS))
    slope = slope.reshape(512, 512)
    return dict(
        far=halves(far),
        far_back=halves(far.T),
        edge=halves(edge),
        edge_back=halves(edge_back),
        near=halves(near),
        near_back=halves(near_back),
        side=halves(side),
        side_back=halves(side.T),
        twist_y=twist(y_angle),
        twist_x=twist(x_angle),
        slope=halves(slope),
    )


def dot(a, b):
    return jnp.dot(a, b, preferred_element_type=F32)


def split(x):
    lead = x.astype(BF16)
    return lead, (x - lead.astype(F32)).astype(BF16)


def from_left(table, x):
    lead, rest = split(x)
    width = x.shape[1]
    both = dot(table[0], jnp.concatenate([lead, rest], 1))
    return both[:, :width] + both[:, width:] + dot(table[1], lead)


def from_right(x, table):
    lead, rest = split(x)
    rows = x.shape[0]
    both = dot(jnp.concatenate([lead, rest], 0), table[0])
    return both[:rows] + both[rows:] + dot(lead, table[1])


def slot_zero(shape):
    return lax.broadcasted_iota(jnp.int32, shape, 1) % 128 < 16


def y_forward(t, field):
    parts = from_right(field, t["near"])
    re, im = parts[:, :128], parts[:, 128:]
    c, s = t["twist_y"][0], t["twist_y"][1]
    parts = jnp.concatenate([re * c - im * s, re * s + im * c], 0)
    usual = from_left(t["far"], parts)
    first = from_left(t["edge"], parts)
    out = jnp.where(slot_zero(usual.shape), first, usual)
    return out[:128], out[128:]


def y_back(t, re, im):
    parts = jnp.concatenate([re, im], 0)
    usual = from_left(t["far_back"], parts)
    first = from_left(t["edge_back"], parts)
    parts = jnp.where(slot_zero(usual.shape), first, usual)
    re, im = parts[:128], parts[128:]
    c, s = t["twist_y"][0], t["twist_y"][1]
    parts = jnp.concatenate([re * c + im * s, im * c - re * s], 1)
    return from_right(parts, t["near_back"])


def x_forward(t, re, im, mirrored):
    parts = jnp.concatenate([re, im], 0)
    if mirrored:
        parts = jnp.concatenate([parts, jnp.concatenate([re, -im], 0)], 1)
    parts = from_left(t["far"], parts)
    c, s = t["twist_x"][0], t["twist_x"][1]
    rows = []
    for at in range(0, parts.shape[1], 128):
        re, im = parts[:128, at : at + 128], parts[128:, at : at + 128]
        rows.append(jnp.concatenate([re * c - im * s, re * s + im * c], 1))
    parts = from_right(jnp.concatenate(rows, 0) if mirrored else rows[0], t["side"])
    out = parts[:128, :128], parts[:128, 128:]
    if mirrored:
        out += parts[128:, :128], parts[128:, 128:]
    return out


def x_back(t, re, im):
    parts = from_right(jnp.concatenate([re, im], 1), t["side_back"])
    re, im = parts[:, :128], parts[:, 128:]
    c, s = t["twist_x"][0], t["twist_x"][1]
    parts = jnp.concatenate([re * c + im * s, im * c - re * s], 0)
    out = from_left(t["far_back"], parts)
    return out[:128], out[128:]


def x_waves():
    q1 = lax.broadcasted_iota(jnp.int32, (128, 128), 0)
    lane = lax.broadcasted_iota(jnp.int32, (128, 128), 1)
    kx = q1 + 128 * (lane % 16)
    return jnp.where(kx < NS // 2, kx, kx - NS)


def odd_x():
    kx = x_waves()
    return jnp.where(kx == -(NS // 2), 0, kx).astype(F32) * WAVE_UNIT


def squared_waves(device):
    slot = lax.broadcasted_iota(jnp.int32, (128, 128), 1) // 16
    first = jnp.where(device < 64, 16 * device, 8 + 16 * (device - 64))
    ky = jnp.where(slot == 0, first, slot + 16 * device)
    other = jnp.where((slot == 0) & (device == 0), NS // 2, ky)
    fold = lambda k: jnp.where(k > NS // 2, NS - k, k).astype(F32) * WAVE_UNIT
    wave_x = x_waves().astype(F32) * WAVE_UNIT
    return wave_x * wave_x + fold(ky) * fold(ky), wave_x * wave_x + fold(other) * fold(other)


def even_filter(spectrum, on_re, on_im):
    re, im, mirror_re, mirror_im = spectrum
    plus = (on_re + on_im) * (0.5 / (NS * NS))
    minus = (on_re - on_im) * (0.5 / (NS * NS))
    return re * plus + mirror_re * minus, im * plus + mirror_im * minus


def power_filter(spectrum, squares, power):
    factors = []
    for square in squares:
        magnitude = jnp.sqrt(square)
        factors.append({1: magnitude, 2: square, 3: square * magnitude}[power])
    return even_filter(spectrum, *factors)


def x_derivative(re, im, scale):
    factor = odd_x() * scale
    return -factor * im, factor * re


def y_derivative(re, im):
    d = lax.broadcasted_iota(jnp.int32, (128, 128), 0)
    slot = lax.broadcasted_iota(jnp.int32, (128, 128), 1) // 16
    first = jnp.where(d < 64, 16 * d, 8 + 16 * (d - 64))
    ky = jnp.where(slot == 0, first, slot + 16 * d)
    factor = jnp.where(ky < NS // 2, ky, ky - NS).astype(F32) * (WAVE_UNIT / NS)
    return -factor * im, factor * re


def to_lanes(rows):
    return jnp.concatenate([rows[:, 128 * a : 128 * a + 128] for a in range(16)], 0).T


def pick(ref, fields, index):
    step = 2 * fields
    return ref[pl.ds(2 * index, 128, step), :], ref[pl.ds(2 * index + 1, 128, step), :]


def put(ref, fields, index, values):
    step = 2 * fields
    ref[pl.ds(2 * index, 128, step), :] = values[0]
    ref[pl.ds(2 * index + 1, 128, step), :] = values[1]


def run(body, names, outs, *arrays, scalars=None, scratch=()):
    consts = [jnp.asarray(tables()[name]) for name in names]
    lead = [] if scalars is None else [scalars]

    def kernel(*refs):
        at = len(lead)
        held = dict(zip(names, refs[at : at + len(names)]))
        body(held, *refs[:at], *refs[at + len(names) :])

    vmem = pl.BlockSpec(memory_space=pltpu.VMEM)
    smem = pl.BlockSpec(memory_space=pltpu.SMEM)
    return pl.pallas_call(
        kernel,
        out_shape=[jax.ShapeDtypeStruct(shape, F32) for shape in outs],
        in_specs=[smem] * len(lead) + [vmem] * (len(consts) + len(arrays)),
        out_specs=[vmem] * len(outs),
        scratch_shapes=list(scratch),
        name=body.__name__,
    )(*lead, *consts, *arrays)


Y_FWD = ("near", "far", "edge", "twist_y")
Y_BACK = ("near_back", "far_back", "edge_back", "twist_y")
Y_BOTH = ("near", "far", "edge", "twist_y", "near_back", "far_back", "edge_back")
X_BOTH = ("far", "side", "twist_x", "far_back", "side_back")
X_BACK = ("twist_x", "far_back", "side_back")
PLANES = (256, 128)
FIELD = (128, 256)


def rows_start(t, phi, send, speed):
    spectrum = y_forward(t, to_lanes(phi[...]))
    put(send, 1, 0, spectrum)
    speed[...] = y_back(t, *y_derivative(*spectrum))


def rows_surface(t, eta, send, lanes, slope):
    lanes[...] = to_lanes(eta[...])
    spectrum = y_forward(t, lanes[...])
    put(send, 1, 0, spectrum)
    slope[...] = y_back(t, *y_derivative(*spectrum))


def columns_first(t, device, got, send, later):
    spectrum = x_forward(t, *pick(got, 1, 0), True)
    squares = squared_waves(device[0])
    put(send, 2, 0, x_back(t, *power_filter(spectrum, squares, 1)))
    put(send, 2, 1, x_back(t, *power_filter(spectrum, squares, 2)))
    put(later, 2, 0, power_filter(spectrum, squares, 3))
    put(later, 2, 1, x_derivative(spectrum[0], spectrum[1], 1.0 / (NS * NS)))


def columns_later(t, held, send):
    for index in range(2):
        put(send, 2, index, x_back(t, *pick(held, 2, index)))


def rows_second(t, got, lanes, surface, send, once, twice):
    once[...] = y_back(t, *pick(got, 2, 0))
    put(send, 2, 0, y_forward(t, -lanes[...] * once[...]))
    put(send, 2, 1, pick(surface, 1, 0))
    twice[...] = y_back(t, *pick(got, 2, 1))


def columns_second(t, device, got, later, send, slope):
    spectrum = x_forward(t, *pick(got, 2, 0), True)
    squares = squared_waves(device[0])
    put(send, 4, 0, x_back(t, *power_filter(spectrum, squares, 1)))
    put(send, 4, 1, x_back(t, *power_filter(spectrum, squares, 2)))
    put(send, 4, 2, pick(later, 2, 0))
    put(send, 4, 3, pick(later, 2, 1))
    re, im = x_forward(t, *pick(got, 2, 1), False)
    put(slope, 1, 0, x_back(t, *x_derivative(re, im, 1.0 / (NS * NS))))


def rows_third(t, got, lanes, once, twice, send, sums, speed):
    eta = lanes[...]
    second_once = y_back(t, *pick(got, 4, 0))
    third = -eta * second_once - 0.5 * eta * eta * twice[...]
    put(send, 1, 0, y_forward(t, third))
    second_twice = y_back(t, *pick(got, 4, 1))
    thrice = y_back(t, *pick(got, 4, 2))
    speed[...] = y_back(t, *pick(got, 4, 3))
    sums[...] = (
        once[...]
        + eta * twice[...]
        + 0.5 * eta * eta * thrice
        + second_once
        + eta * second_twice
    )


def columns_third(t, device, got, slope, send):
    spectrum = x_forward(t, *pick(got, 1, 0), True)
    put(send, 2, 0, x_back(t, *power_filter(spectrum, squared_waves(device[0]), 1)))
    put(send, 2, 1, pick(slope, 1, 0))


def rows_finish(t, got, lanes, sums, speed_x, speed_y, slope_y, new_rows, send, window):
    third_once = y_back(t, *pick(got, 2, 0))
    slope_x = y_back(t, *pick(got, 2, 1))
    eta, along = lanes[...], slope_y[...]
    tendency = -(slope_x * speed_x[...] + along * speed_y[...]) + (
        1.0 + slope_x * slope_x + along * along
    ) * (sums[...] + third_once)
    new = (eta + DT_WAVE * tendency).T
    for a in range(16):
        new_rows[:, 128 * a : 128 * a + 128] = new[16 * a : 16 * a + 16]
    window[0:32, :] = new[:32]
    window[32:64, :] = eta.T[:32]
    group = lax.broadcasted_iota(jnp.int32, (16, 128), 1) // 32
    blocks = []
    for a in range(2):
        rows = new[16 * a : 16 * a + 16]
        turned = [rows] + [pltpu.roll(rows, 32 * k, 1) for k in range(1, 4)]
        for chunk in range(4):
            block = jnp.zeros((4, 128), F32)
            for g in range(4):
                moved = turned[(g - chunk) % 4]
                block = block + jnp.where(group == g, moved, 0.0)[4 * g : 4 * g + 4]
            blocks.append(block)
    block = jnp.concatenate(blocks, 0)
    for at in range(16):
        send[32 * at : 32 * at + 32, :] = block


def columns_slope(t, slab, got, window, send, twofold):
    twofold[0:512, :] = got[...]
    twofold[512:1024, :] = got[...]
    start = pl.multiple_of(slab[0] * 32, 32)
    full = from_left(t["slope"], twofold[pl.ds(start, 512), :])
    group = lax.broadcasted_iota(jnp.int32, (128, 128), 1) // 32
    total = jnp.zeros((128, 128), F32)
    for g in range(4):
        total = total + jnp.where(group == g, full[128 * g : 128 * g + 128], 0.0)
    total = total + pltpu.roll(total, 64, 1)
    total = total + pltpu.roll(total, 32, 1)
    slope = total.T[:32]
    for at in range(8):
        send[96 * at : 96 * at + 32, :] = slope
        send[96 * at + 32 : 96 * at + 96, :] = window[...]


def air_finish(got, moved, wind, below, above, place, out, slope_s, new_s, old_s):
    step = pl.program_id(0)
    depth = out.shape[0]

    @pl.when(step == 0)
    def _():
        slope_t = jnp.concatenate([got[96 * g : 96 * g + 32, :] for g in range(8)], 0)
        slope_s[...] = slope_t.T
        for g in range(8):
            for a in range(2):
                at = 96 * g + 32 + 16 * a
                rows, lanes = slice(16 * g, 16 * g + 16), slice(128 * a, 128 * a + 128)
                new_s[rows, lanes] = got[at : at + 16, :]
                old_s[rows, lanes] = got[at + 32 : at + 48, :]

    here = pl.ds(pl.multiple_of(step * depth, depth), depth)
    slope, new, old = slope_s[here, :], new_s[here, :], old_s[here, :]
    group, levels = place[0], moved.shape[1]
    total = levels * place[1]
    ratio = (new - old) / (COLUMN_DEPTH - old) * total.astype(F32)
    inverse = 1.0 / (COLUMN_DEPTH - new)
    level = lax.broadcasted_iota(jnp.int32, (levels, 256), 0)
    lift = 1.0 - ((group * levels + level).astype(F32) + 0.5) / total.astype(F32)
    lift_below = 1.0 - ((group * levels - 1).astype(F32) + 0.5) / total.astype(F32)
    lift_above = 1.0 - ((group * levels + levels).astype(F32) + 0.5) / total.astype(F32)
    bottom, top = group == 0, group == place[1] - 1

    def remap(lower, mid, upper, shift):
        return (
            mid + 0.5 * shift * (upper - lower) + 0.5 * shift * shift * (upper - 2.0 * mid + lower)
        )

    advect = slope * inverse * (DT_AIR * 0.5 * total.astype(F32))
    spread = inverse * inverse * (DT_AIR * NU_AIR * (total * total).astype(F32))
    for x in range(depth):
        row = slice(x, x + 1)
        m = moved[x]
        outer_low, low = below[x, 0:1], below[x, 1:2]
        high, outer_high = above[x, 0:1], above[x, 1:2]
        low = jnp.where(bottom, m[:1], low)
        high = jnp.where(top, m[levels - 1 :], high)
        lower = jnp.where(level == 0, low, pltpu.roll(m, 1, 0))
        upper = jnp.where(level == levels - 1, high, pltpu.roll(m, levels - 1, 0))
        shift = ratio[row] * lift
        r = remap(lower, m, upper, shift)
        r_low = remap(outer_low, low, m[:1], ratio[row] * lift_below)
        r_high = remap(m[levels - 1 :], high, outer_high, ratio[row] * lift_above)
        r_low = jnp.where(bottom, r[:1], r_low)
        r_high = jnp.where(top, r[levels - 1 :], r_high)
        lower = jnp.where(level == 0, r_low, pltpu.roll(r, 1, 0))
        upper = jnp.where(level == levels - 1, r_high, pltpu.roll(r, levels - 1, 0))
        out[x] = (
            r
            + wind[x] * lift * advect[row] * (upper - lower)
            + spread[row] * (upper - 2.0 * r + lower)
        )


def air_call(got, moved, wind, below, above, place):
    depth = 16
    block = pl.BlockSpec((depth, 8, 256), lambda i: (i, 0, 0))
    rim = pl.BlockSpec((depth, 2, 256), lambda i: (i, 0, 0))
    return pl.pallas_call(
        air_finish,
        out_shape=jax.ShapeDtypeStruct(moved.shape, F32),
        grid=(moved.shape[0] // depth,),
        in_specs=[
            pl.BlockSpec(got.shape, lambda i: (0, 0)),
            block,
            block,
            rim,
            rim,
            pl.BlockSpec(memory_space=pltpu.SMEM),
        ],
        out_specs=block,
        scratch_shapes=[pltpu.VMEM((128, 256), F32)] * 3,
        name="air_finish",
    )(got, moved, wind, below, above, place)


def moved_air(tracer, wind_speed):
    size = lax.axis_size("gx")
    up = [(i, (i + 1) % size) for i in range(size)]
    down = [(j, i) for i, j in up]
    before = lax.ppermute(tracer[-1:], "gx", up)
    after = lax.ppermute(tracer[:1], "gx", down)
    western = jnp.concatenate([before, tracer[:-1]], 0)
    eastern = jnp.concatenate([tracer[1:], after], 0)
    northern = jnp.concatenate([tracer[:, :, 1:], tracer[:, :, -1:]], 2)
    southern = jnp.concatenate([tracer[:, :, :1], tracer[:, :, :-1]], 2)
    moved = tracer + DT_AIR * (
        -wind_speed * (eastern - western) * 0.5
        + NU_AIR * (eastern + western + northern + southern - 4.0 * tracer)
    )
    size = lax.axis_size("gz")
    up = [(i, i + 1) for i in range(size - 1)]
    down = [(j, i) for i, j in up]
    below = lax.ppermute(moved[:, -2:], "gz", up)
    above = lax.ppermute(moved[:, :2], "gz", down)
    return moved, below, above


def exchange(buffer, axes=BOTH):
    return lax.all_to_all(buffer, axes, split_axis=0, concat_axis=0, tiled=True)


def shards(elevation, potential, tracer, wind_speed):
    gx, gz = lax.axis_index("gx"), lax.axis_index("gz")
    device = (gx * lax.axis_size("gz") + gz).astype(jnp.int32).reshape(1)
    slab = gx.astype(jnp.int32).reshape(1)
    place = jnp.stack([gz, lax.axis_size("gz")]).astype(jnp.int32)

    send, speed_y = run(rows_start, Y_BOTH, [PLANES, FIELD], potential)
    got = exchange(send)
    surface, lanes, slope_y = run(rows_surface, Y_BOTH, [PLANES, FIELD, FIELD], elevation)
    moved, below, above = moved_air(tracer, wind_speed)

    send, later = run(columns_first, X_BOTH, [(512, 128), (512, 128)], got, scalars=device)
    got = exchange(send)
    (later,) = run(columns_later, X_BACK, [(512, 128)], later)

    send, once, twice = run(
        rows_second, Y_BOTH, [(512, 128), FIELD, FIELD], got, lanes, surface
    )
    got = exchange(send)
    send, slope = run(columns_second, X_BOTH, [(1024, 128), PLANES], got, later, scalars=device)
    got = exchange(send)
    send, sums, speed_x = run(
        rows_third, Y_BOTH, [PLANES, FIELD, FIELD], got, lanes, once, twice
    )
    got = exchange(send)
    (send,) = run(columns_third, X_BOTH, [(512, 128)], got, slope, scalars=device)
    got = exchange(send)
    new_rows, send, window = run(
        rows_finish,
        Y_BACK,
        [(16, NS), (512, 128), (64, 128)],
        got,
        lanes,
        sums,
        speed_x,
        speed_y,
        slope_y,
    )
    got = exchange(send)
    (send,) = run(
        columns_slope,
        ("slope",),
        [(768, 128)],
        got,
        window,
        scalars=slab,
        scratch=[pltpu.VMEM((1024, 128), F32)],
    )
    got = exchange(send, "gz")
    return new_rows, air_call(got, moved, wind_speed, below, above, place)


def solution(mesh):
    return jax.shard_map(
        shards,
        mesh=mesh,
        in_specs=(P(BOTH, None), P(BOTH, None), P("gx", "gz", None), P("gx", "gz", None)),
        out_specs=(P(BOTH, None), P("gx", "gz", None)),
        check_vma=False,
    )
```

```python
import functools

import jax
import jax.numpy as jnp
import ml_dtypes
import numpy as np
from jax import lax
from jax.experimental import pallas as pl
from jax.experimental.pallas import tpu as pltpu
from jax.sharding import PartitionSpec as P

NS = 2048
DT_WAVE = 0.05
COLUMN_DEPTH = 32.0
DT_AIR = 0.1
NU_AIR = 0.2
TWO_PI = 6.283185307179586
WAVE_UNIT = TWO_PI / NS
BOTH = ("gx", "gz")
F32 = jnp.float32
BF16 = jnp.bfloat16


def halves(matrix):
    exact = np.asarray(matrix, np.float64)
    lead = exact.astype(np.float32).astype(ml_dtypes.bfloat16)
    rest = (exact - lead.astype(np.float64)).astype(np.float32).astype(ml_dtypes.bfloat16)
    return np.stack([lead, rest])


@functools.cache
def tables():
    n128, n16 = np.arange(128), np.arange(16)
    eye16, eye8 = np.eye(16), np.eye(8)
    turn = 2 * np.pi * (np.outer(n128, n128) % 128) / 128
    c, s = np.cos(turn), np.sin(turn)
    wheel = np.concatenate([c, s], 0)
    edge = np.zeros((2, 128, 2, 128))
    edge_back = np.zeros((2, 128, 2, 128))
    sign = (-1.0) ** n128
    for d in range(128):
        if d < 64:
            angle, part = 2 * np.pi * n128 * d / 128, 0
        else:
            angle, part = 2 * np.pi * n128 * (2 * (d - 64) + 1) / 256, 1
        edge[0, d, part] = np.cos(angle)
        edge[1, d, part] = -np.sin(angle) if d else sign
        weight = 2.0 if d else 1.0
        edge_back[part, :, 0, d] = weight * np.cos(angle)
        edge_back[part, :, 1, d] = -weight * np.sin(angle) if d else sign
    edge = edge.reshape(256, 256)
    edge_back = edge_back.reshape(256, 256)
    k8 = np.arange(8)
    angle = 2 * np.pi * np.outer(n16, k8) / 16
    near_re, near_im = np.cos(angle), -np.sin(angle)
    near_im[:, 0] = (-1.0) ** n16
    weight = np.where(k8 == 0, 1.0, 2.0)
    near = np.zeros((16, 16, 2, 8, 16))
    near_back = np.zeros((2, 8, 16, 16, 16))
    for part, table in enumerate((near_re, near_im)):
        near[:, :, part] = table[:, None, :, None] * eye16[None, :, None, :]
        near_back[part] = (table * weight).T[:, None, :, None] * eye16[None, :, None, :]
    near = near.reshape(256, 256)
    near_back = near_back.reshape(256, 256)
    angle = 2 * np.pi * np.outer(n16, n16) / 16
    cx, sx = np.kron(eye8, np.cos(angle)), np.kron(eye8, np.sin(angle))
    comb = np.concatenate([cx, sx], 0)
    y_angle = 2 * np.pi * np.repeat(np.outer(n128, k8), 16, axis=1) / NS
    x_angle = 2 * np.pi * np.tile(np.outer(n128, n16), (1, 8)) / NS
    twist = lambda a: np.stack([np.cos(a), -np.sin(a)]).astype(np.float32)
    r = n128[None, :, None, None]
    x = 16 * n128[None, None, :, None] + n16.reshape(4, 1, 1, 4)
    n = r - x
    with np.errstate(divide="ignore", invalid="ignore"):
        slope = np.where(n % NS == 0, 0.0, (np.pi / NS) * (-1.0) ** (n % 2) / np.tan(np.pi * n / NS))
    slope = slope.reshape(512, 512)
    return dict(
        wheel=halves(wheel),
        edge=halves(edge),
        edge_back=halves(edge_back),
        near=halves(near),
        near_back=halves(near_back),
        comb=halves(comb),
        twist_y=twist(y_angle),
        twist_x=twist(x_angle),
        slope=halves(slope),
    )


def dot(a, b):
    return jnp.dot(a, b, preferred_element_type=F32)


def split(x):
    lead = x.astype(BF16)
    return lead, (x - lead.astype(F32)).astype(BF16)


def from_left(table, x):
    lead, rest = split(x)
    width = x.shape[1]
    both = dot(table[0], jnp.concatenate([lead, rest], 1))
    return both[:, :width] + both[:, width:] + dot(table[1], lead)


def from_right(x, table):
    lead, rest = split(x)
    rows = x.shape[0]
    both = dot(jnp.concatenate([lead, rest], 0), table[0])
    return both[:rows] + both[rows:] + dot(lead, table[1])


def turning(table, sign):
    blocks = []
    for half in (table[0], table[1]):
        c, s = half[:128], half[128:]
        upper, lower = (s, -s) if sign > 0 else (-s, s)
        rows = [jnp.concatenate([c, upper], 1), jnp.concatenate([lower, c], 1)]
        blocks.append(jnp.concatenate(rows, 0))
    return blocks


def slot_zero(shape):
    return lax.broadcasted_iota(jnp.int32, shape, 1) % 128 < 16


def y_forward(t, field):
    parts = from_right(field, t["near"])
    re, im = parts[:, :128], parts[:, 128:]
    c, s = t["twist_y"][0], t["twist_y"][1]
    parts = jnp.concatenate([re * c - im * s, re * s + im * c], 0)
    usual = from_left(turning(t["wheel"], 1), parts)
    first = from_left(t["edge"], parts)
    out = jnp.where(slot_zero(usual.shape), first, usual)
    return out[:128], out[128:]


def y_back_far(t, re, im):
    parts = jnp.concatenate([re, im], 0)
    usual = from_left(turning(t["wheel"], -1), parts)
    first = from_left(t["edge_back"], parts)
    parts = jnp.where(slot_zero(usual.shape), first, usual)
    c, s = t["twist_y"][0], t["twist_y"][1]
    out = []
    for at in range(0, parts.shape[1], 128):
        re, im = parts[:128, at : at + 128], parts[128:, at : at + 128]
        out.append(jnp.concatenate([re * c + im * s, im * c - re * s], 1))
    return out


def y_back(t, re, im):
    return from_right(y_back_far(t, re, im)[0], t["near_back"])


def x_forward(t, re, im, mirrored):
    parts = jnp.concatenate([re, im], 0)
    if mirrored:
        parts = jnp.concatenate([parts, jnp.concatenate([re, -im], 0)], 1)
    parts = from_left(turning(t["wheel"], 1), parts)
    c, s = t["twist_x"][0], t["twist_x"][1]
    rows = []
    for at in range(0, parts.shape[1], 128):
        re, im = parts[:128, at : at + 128], parts[128:, at : at + 128]
        rows.append(jnp.concatenate([re * c - im * s, re * s + im * c], 1))
    parts = from_right(jnp.concatenate(rows, 0) if mirrored else rows[0], turning(t["comb"], -1))
    out = parts[:128, :128], parts[:128, 128:]
    if mirrored:
        out += parts[128:, :128], parts[128:, 128:]
    return out


def x_back(t, re, im):
    parts = from_right(jnp.concatenate([re, im], 1), turning(t["comb"], 1))
    re, im = parts[:, :128], parts[:, 128:]
    c, s = t["twist_x"][0], t["twist_x"][1]
    parts = jnp.concatenate([re * c + im * s, im * c - re * s], 0)
    out = from_left(turning(t["wheel"], -1), parts)
    return out[:128], out[128:]


def x_waves():
    q1 = lax.broadcasted_iota(jnp.int32, (128, 128), 0)
    lane = lax.broadcasted_iota(jnp.int32, (128, 128), 1)
    kx = q1 + 128 * (lane % 16)
    return jnp.where(kx < NS // 2, kx, kx - NS)


def odd_x():
    kx = x_waves()
    return jnp.where(kx == -(NS // 2), 0, kx).astype(F32) * WAVE_UNIT


def squared_waves(device):
    slot = lax.broadcasted_iota(jnp.int32, (128, 128), 1) // 16
    first = jnp.where(device < 64, 16 * device, 8 + 16 * (device - 64))
    ky = jnp.where(slot == 0, first, slot + 16 * device)
    other = jnp.where((slot == 0) & (device == 0), NS // 2, ky)
    fold = lambda k: jnp.where(k > NS // 2, NS - k, k).astype(F32) * WAVE_UNIT
    wave_x = x_waves().astype(F32) * WAVE_UNIT
    return wave_x * wave_x + fold(ky) * fold(ky), wave_x * wave_x + fold(other) * fold(other)


def even_filter(spectrum, on_re, on_im):
    re, im, mirror_re, mirror_im = spectrum
    plus = (on_re + on_im) * (0.5 / (NS * NS))
    minus = (on_re - on_im) * (0.5 / (NS * NS))
    return re * plus + mirror_re * minus, im * plus + mirror_im * minus


def power_filter(spectrum, squares, power):
    factors = []
    for square in squares:
        magnitude = jnp.sqrt(square)
        factors.append({1: magnitude, 2: square, 3: square * magnitude}[power])
    return even_filter(spectrum, *factors)


def x_derivative(re, im, scale):
    factor = odd_x() * scale
    return -factor * im, factor * re


def y_derivative(re, im):
    d = lax.broadcasted_iota(jnp.int32, (128, 128), 0)
    slot = lax.broadcasted_iota(jnp.int32, (128, 128), 1) // 16
    first = jnp.where(d < 64, 16 * d, 8 + 16 * (d - 64))
    ky = jnp.where(slot == 0, first, slot + 16 * d)
    factor = jnp.where(ky < NS // 2, ky, ky - NS).astype(F32) * (WAVE_UNIT / NS)
    return -factor * im, factor * re


def to_lanes(rows):
    return jnp.concatenate([rows[:, 128 * a : 128 * a + 128] for a in range(16)], 0).T


def pick(ref, fields, index):
    step = 2 * fields
    return ref[pl.ds(2 * index, 128, step), :], ref[pl.ds(2 * index + 1, 128, step), :]


def put(ref, fields, index, values):
    step = 2 * fields
    ref[pl.ds(2 * index, 128, step), :] = values[0]
    ref[pl.ds(2 * index + 1, 128, step), :] = values[1]


def near_core(array):
    return pltpu.with_memory_space_constraint(array, pltpu.VMEM)


def far_away(array):
    return pltpu.with_memory_space_constraint(array, pltpu.HBM)


def run(body, names, outs, *arrays, held, scalars=None, scratch=(), far=()):
    consts = [near_core(held[name]) for name in names]
    lead = [] if scalars is None else [scalars]
    arrays = [far_away(a) if i in far else near_core(a) for i, a in enumerate(arrays)]

    def kernel(*refs):
        at = len(lead)
        tabs = dict(zip(names, refs[at : at + len(names)]))
        body(tabs, *refs[:at], *refs[at + len(names) :])

    vmem = pl.BlockSpec(memory_space=pltpu.VMEM)
    smem = pl.BlockSpec(memory_space=pltpu.SMEM)
    place = lambda out: (pltpu.VMEM if out[-1] == "near" else pltpu.HBM)(out[:2], F32)
    return pl.pallas_call(
        kernel,
        out_shape=[place(out) for out in outs],
        in_specs=[smem] * len(lead) + [vmem] * (len(consts) + len(arrays)),
        out_specs=[vmem] * len(outs),
        scratch_shapes=list(scratch),
        compiler_params=pltpu.CompilerParams(vmem_limit_bytes=16 << 20),
    )(*lead, *consts, *arrays)


Y_FWD = ("near", "wheel", "edge", "twist_y")
Y_BACK = ("near_back", "wheel", "edge_back", "twist_y")
Y_BOTH = ("near", "wheel", "edge", "twist_y", "near_back", "edge_back")
X_BOTH = ("wheel", "comb", "twist_x")
PLANES = (256, 128)
FIELD = (128, 256, "near")
NAMES = ("wheel", "comb", "twist_x", "near", "near_back", "edge", "edge_back", "twist_y")


def copied(names, arrays, body, outs, keep):
    sources = [jnp.asarray(tables()[name]) for name in names] + list(arrays)
    count, kept = len(sources), len(names) if keep else 0

    def kernel(*refs):
        sems = refs[-1]
        inputs, results = refs[:count], refs[count : count + len(outs)]
        targets = refs[count + len(outs) : -1]
        copies = [pltpu.make_async_copy(inputs[i], targets[i], sems.at[i]) for i in range(count)]
        for copy in copies:
            copy.start()
        for copy in copies:
            copy.wait()
        if body is not None:
            body(dict(zip(names, targets)), *targets[len(names) :], *results)

    vmem = pl.BlockSpec(memory_space=pltpu.VMEM)
    return pl.pallas_call(
        kernel,
        out_shape=[pltpu.HBM(out[:2], F32) for out in outs]
        + [pltpu.VMEM(c.shape, c.dtype) for c in sources[:kept]],
        in_specs=[pl.BlockSpec(memory_space=pltpu.HBM)] * count,
        out_specs=[vmem] * (len(outs) + kept),
        scratch_shapes=[pltpu.VMEM(c.shape, c.dtype) for c in sources[kept:]]
        + [pltpu.SemaphoreType.DMA((count,))],
        compiler_params=pltpu.CompilerParams(vmem_limit_bytes=16 << 20),
    )(*[far_away(source) for source in sources])


def hold_tables():
    return dict(zip(NAMES, copied(NAMES, (), None, (), True)))


def stacked(ref):
    return [ref[128 * i : 128 * i + 128, :] for i in range(ref.shape[0] // 128)]


def rows_start(t, phi, send):
    put(send, 1, 0, y_forward(t, to_lanes(phi[...])))


def rows_surface(t, eta, start, send, lanes, slope, speed):
    lanes[...] = to_lanes(eta[...])
    spectrum = y_forward(t, lanes[...])
    put(send, 1, 0, spectrum)
    slope[...] = y_back(t, *y_derivative(*spectrum))
    speed[...] = y_back(t, *y_derivative(*pick(start, 1, 0)))


def columns_first(t, device, got, send, held):
    spectrum = x_forward(t, *pick(got, 1, 0), True)
    for i, part in enumerate(spectrum):
        held[128 * i : 128 * i + 128, :] = part
    put(send, 1, 0, x_back(t, *power_filter(spectrum, squared_waves(device[0]), 1)))


def columns_first_late(t, device, held, late):
    spectrum = stacked(held)
    squares = squared_waves(device[0])
    put(late, 3, 0, x_back(t, *power_filter(spectrum, squares, 2)))
    put(late, 3, 1, x_back(t, *power_filter(spectrum, squares, 3)))
    put(late, 3, 2, x_back(t, *x_derivative(spectrum[0], spectrum[1], 1.0 / (NS * NS))))


def rows_second(t, got, lanes, surface, send, once):
    once[...] = y_back(t, *pick(got, 1, 0))
    put(send, 2, 0, y_forward(t, -lanes[...] * once[...]))
    put(send, 2, 1, pick(surface, 1, 0))


def columns_second(t, device, got, late, send, held):
    spectrum = x_forward(t, *pick(got, 2, 0), True)
    for i, part in enumerate(spectrum):
        held[128 * i : 128 * i + 128, :] = part
    for i, part in enumerate(pick(got, 2, 1)):
        held[512 + 128 * i : 640 + 128 * i, :] = part
    put(send, 4, 0, x_back(t, *power_filter(spectrum, squared_waves(device[0]), 1)))
    for index in range(3):
        put(send, 4, 1 + index, pick(late, 3, index))


def columns_second_late(t, device, held, late):
    parts = stacked(held)
    put(late, 2, 0, x_back(t, *power_filter(parts[:4], squared_waves(device[0]), 2)))
    re, im = x_forward(t, parts[4], parts[5], False)
    put(late, 2, 1, x_back(t, *x_derivative(re, im, 1.0 / (NS * NS))))


def rows_third(t, got, lanes, send, once, twice):
    eta = lanes[...]
    once[...] = y_back(t, *pick(got, 4, 0))
    twice[...] = y_back(t, *pick(got, 4, 1))
    third = -eta * once[...] - 0.5 * eta * eta * twice[...]
    put(send, 1, 0, y_forward(t, third))


def rows_third_late(t, got, lanes, first_once, once, twice, sums, speed):
    eta = lanes[...]
    thrice = y_back(t, *pick(got, 4, 2))
    speed[...] = y_back(t, *pick(got, 4, 3))
    sums[...] = first_once[...] + eta * twice[...] + 0.5 * eta * eta * thrice + once[...]


def columns_third(t, device, got, late, send):
    spectrum = x_forward(t, *pick(got, 1, 0), True)
    put(send, 3, 0, x_back(t, *power_filter(spectrum, squared_waves(device[0]), 1)))
    for index in range(2):
        put(send, 3, 1 + index, pick(late, 2, index))


def finished(t, parts, lanes, sums, speed_x, speed_y, slope_y, width):
    near = [half[:, :width] for half in (t["near_back"][0], t["near_back"][1])]
    back = from_right(jnp.concatenate(parts, 0), near)
    third_once, second_twice, slope_x = back[:128], back[128:256], back[256:]
    eta, along = lanes[:, :width], slope_y[:, :width]
    tendency = -(slope_x * speed_x[:, :width] + along * speed_y[:, :width]) + (
        1.0 + slope_x * slope_x + along * along
    ) * (sums[:, :width] + third_once + eta * second_twice)
    return eta + DT_WAVE * tendency


def rows_finish(t, got, lanes, sums, speed_x, speed_y, slope_y, parts_out, send, window):
    parts = y_back_far(t, *[jnp.concatenate(p, 1) for p in zip(*[pick(got, 3, i) for i in range(3)])])
    for i, part in enumerate(parts):
        parts_out[128 * i : 128 * i + 128, :] = part
    new = finished(t, parts, lanes, sums, speed_x, speed_y, slope_y, 128).T[:32]
    window[0:32, :] = new
    window[32:64, :] = lanes[:, 0:128].T[:32]
    group = lax.broadcasted_iota(jnp.int32, (16, 128), 1) // 32
    blocks = []
    for a in range(2):
        rows = new[16 * a : 16 * a + 16]
        turned = [rows] + [pltpu.roll(rows, 32 * k, 1) for k in range(1, 4)]
        for chunk in range(4):
            block = jnp.zeros((4, 128), F32)
            for g in range(4):
                moved = turned[(g - chunk) % 4]
                block = block + jnp.where(group == g, moved, 0.0)[4 * g : 4 * g + 4]
            blocks.append(block)
    block = jnp.concatenate(blocks, 0)
    for at in range(16):
        send[32 * at : 32 * at + 32, :] = block


def rows_output(t, parts, lanes, sums, speed_x, speed_y, slope_y, new_rows):
    parts = [parts[128 * i : 128 * i + 128, :] for i in range(3)]
    new = finished(t, parts, lanes, sums, speed_x, speed_y, slope_y, 256).T
    for a in range(16):
        new_rows[:, 128 * a : 128 * a + 128] = new[16 * a : 16 * a + 16]


def columns_slope(t, slab, got, window, table, send, twofold):
    twofold[0:512, :] = got[...]
    twofold[512:1024, :] = got[...]
    start = pl.multiple_of(slab[0] * 32, 32)
    full = from_left(table, twofold[pl.ds(start, 512), :])
    group = lax.broadcasted_iota(jnp.int32, (128, 128), 1) // 32
    total = jnp.zeros((128, 128), F32)
    for g in range(4):
        total = total + jnp.where(group == g, full[128 * g : 128 * g + 128], 0.0)
    total = total + pltpu.roll(total, 64, 1)
    total = total + pltpu.roll(total, 32, 1)
    slope = total.T[:32]
    for at in range(8):
        send[96 * at : 96 * at + 32, :] = slope
        send[96 * at + 32 : 96 * at + 96, :] = window[...]


def air_moved(t, tracer, wind, before, after, moved, bottom, top):
    levels = before.shape[0]
    count = tracer.shape[0] // levels
    lane = lax.broadcasted_iota(jnp.int32, (levels, 256), 1)

    def put_row(x, west, east):
        at = at_row(x)
        q, w = tracer[at, :], wind[at, :]
        north = jnp.where(lane == 255, q, pltpu.roll(q, 255, 1))
        south = jnp.where(lane == 0, q, pltpu.roll(q, 1, 1))
        q = q + DT_AIR * (
            -w * (east - west) * 0.5 + NU_AIR * (east + west + north + south - 4.0 * q)
        )
        moved[at, :] = q
        for k in range(2):
            bottom[pl.ds(128 * k + x, 1), :] = q[k : k + 1]
            top[pl.ds(128 * k + x, 1), :] = q[levels - 2 + k : levels - 1 + k]

    def at_row(x):
        return pl.ds(pl.multiple_of(x * levels, levels), levels)

    put_row(0, before[...], tracer[at_row(1), :])
    put_row(count - 1, tracer[at_row(count - 2), :], after[...])

    def step(i, carry):
        for k in range(6):
            x = 1 + 6 * i + k
            put_row(x, tracer[at_row(x - 1), :], tracer[at_row(x + 1), :])
        return carry

    lax.fori_loop(0, (count - 2) // 6, step, 0)


def air_finish(place, got, moved, wind, below, above, lowest_rows, highest_rows, out, *scratch):
    ratio_s, inverse_s, spread_s, low_s, high_s, r_low_s, r_high_s = scratch
    block = pl.program_id(0)
    levels = 8
    depth = out.shape[0] // levels
    group, groups = place[0], place[1]
    total = (levels * groups).astype(F32)
    bottom, top = group == 0, group == groups - 1

    def lift_of(level):
        return 1.0 - ((group * levels + level).astype(F32) + 0.5) / total

    def remap(lower, mid, upper, shift):
        return (
            mid + 0.5 * shift * (upper - lower) + 0.5 * shift * shift * (upper - 2.0 * mid + lower)
        )

    @pl.when(block == 0)
    def _():
        slope = jnp.concatenate([got[96 * g : 96 * g + 32, :] for g in range(8)], 0).T
        for g in range(8):
            for a in range(2):
                at = 96 * g + 32 + 16 * a
                rows, lanes = slice(16 * g, 16 * g + 16), slice(128 * a, 128 * a + 128)
                new, old = got[at : at + 16, :], got[at + 32 : at + 48, :]
                ratio_s[rows, lanes] = (new - old) / (COLUMN_DEPTH - old) * total
                inverse = 1.0 / (COLUMN_DEPTH - new)
                inverse_s[rows, lanes] = inverse * (DT_AIR * 0.5 * total) * slope[rows, lanes]
                spread_s[rows, lanes] = inverse * inverse * (DT_AIR * NU_AIR * total * total)
        first, last = lowest_rows[0:128, :], highest_rows[128:256, :]
        low = jnp.where(bottom, first, below[128:256, :])
        high = jnp.where(top, last, above[0:128, :])
        low_s[...], high_s[...] = low, high
        shift = ratio_s[...]
        r_low_s[...] = remap(below[0:128, :], low, first, shift * lift_of(jnp.int32(-1)))
        r_high_s[...] = remap(last, high, above[128:256, :], shift * lift_of(jnp.int32(levels)))

    level = lax.broadcasted_iota(jnp.int32, (levels, 256), 0)
    lift = lift_of(level)
    lowest, highest = level == 0, level == levels - 1

    def step(i, carry):
        for k in range(4):
            x = 4 * i + k
            row = pl.ds(block * depth + x, 1)
            at = pl.ds(pl.multiple_of(x * levels, levels), levels)
            m = moved[at, :]
            lower = jnp.where(lowest, low_s[row, :], pltpu.roll(m, 1, 0))
            upper = jnp.where(highest, high_s[row, :], pltpu.roll(m, levels - 1, 0))
            r = remap(lower, m, upper, ratio_s[row, :] * lift)
            r_low = jnp.where(bottom, r[:1], r_low_s[row, :])
            r_high = jnp.where(top, r[levels - 1 :], r_high_s[row, :])
            lower = jnp.where(lowest, r_low, pltpu.roll(r, 1, 0))
            upper = jnp.where(highest, r_high, pltpu.roll(r, levels - 1, 0))
            out[at, :] = (
                r
                + spread_s[row, :] * (upper - 2.0 * r + lower)
                + wind[at, :] * lift * inverse_s[row, :] * (upper - lower)
            )
        return carry

    lax.fori_loop(0, depth // 4, step, 0)


def air_finish_call(place, got, moved, wind, below, above, bottom, top):
    depth = 16
    rows = pl.BlockSpec((8 * depth, 256), lambda i: (i, 0))
    whole = lambda shape: pl.BlockSpec(shape, lambda i: (0, 0))
    rim = whole((256, 256))
    return pl.pallas_call(
        air_finish,
        out_shape=jax.ShapeDtypeStruct(moved.shape, F32),
        grid=(128 // depth,),
        in_specs=[
            pl.BlockSpec(memory_space=pltpu.SMEM),
            whole((768, 128)),
            rows,
            rows,
            rim,
            rim,
            rim,
            rim,
        ],
        out_specs=rows,
        scratch_shapes=[pltpu.VMEM((128, 256), F32)] * 7,
        compiler_params=pltpu.CompilerParams(vmem_limit_bytes=16 << 20),
        name="air_finish",
    )(place, got, moved, wind, below, above, bottom, top)


def exchange(buffer, axes=BOTH, fields=1):
    if fields == 3:
        buffer = buffer.reshape(128, 3, 2, 128)
    out = lax.all_to_all(buffer, axes, split_axis=0, concat_axis=0, tiled=True)
    return out.reshape(-1, 128)


def shards(elevation, potential, tracer, wind_speed):
    gx, gz = lax.axis_index("gx"), lax.axis_index("gz")
    groups = lax.axis_size("gz")
    device = (gx * groups + gz).astype(jnp.int32).reshape(1)
    slab = gx.astype(jnp.int32).reshape(1)
    place = jnp.concatenate([gz.astype(jnp.int32).reshape(1), jnp.full((1,), groups, jnp.int32)])
    quantity = tracer.reshape(1024, 256)
    wind = wind_speed.reshape(1024, 256)
    size = lax.axis_size("gx")
    ring = [(i, (i + 1) % size) for i in range(size)]
    rise = [(i, i + 1) for i in range(groups - 1)]
    back = lambda pairs: [(j, i) for i, j in pairs]

    (start,) = copied(Y_FWD, [potential], rows_start, [PLANES], False)
    got = exchange(start)
    t = hold_tables()
    surface, lanes, slope_y, speed_y = run(
        rows_surface,
        Y_BOTH,
        [(256, 128, "near"), FIELD, FIELD, FIELD],
        elevation,
        start,
        held=t,
        far=(0, 1),
    )

    send, held = run(
        columns_first, X_BOTH, [PLANES, (512, 128, "near")], got, scalars=device, held=t
    )
    got = exchange(send)
    (late,) = run(columns_first_late, X_BOTH, [(768, 128, "near")], held, scalars=device, held=t)
    before = lax.ppermute(quantity[-8:], "gx", ring)
    after = lax.ppermute(quantity[:8], "gx", back(ring))

    send, first_once = run(rows_second, Y_BOTH, [(512, 128), FIELD], got, lanes, surface, held=t)
    got = exchange(send)
    moved, bottom, top = run(
        air_moved,
        (),
        [(1024, 256), (256, 256), (256, 256)],
        quantity,
        wind,
        before,
        after,
        held=t,
        far=(0, 1, 2, 3),
    )

    send, held = run(
        columns_second,
        X_BOTH,
        [(1024, 128), (768, 128, "near")],
        got,
        late,
        scalars=device,
        held=t,
    )
    got = exchange(send)
    (late,) = run(columns_second_late, X_BOTH, [(512, 128, "near")], held, scalars=device, held=t)
    below = lax.ppermute(top, "gz", rise)
    above = lax.ppermute(bottom, "gz", back(rise))

    send, once, twice = run(rows_third, Y_BOTH, [PLANES, FIELD, FIELD], got, lanes, held=t)
    got_rows, got = got, exchange(send)
    sums, speed_x = run(
        rows_third_late,
        Y_BACK,
        [FIELD, FIELD],
        got_rows,
        lanes,
        first_once,
        once,
        twice,
        held=t,
    )

    (send,) = run(columns_third, X_BOTH, [(768, 128)], got, late, scalars=device, held=t)
    got = exchange(send, fields=3)

    surface_set = (lanes, sums, speed_x, speed_y, slope_y)
    parts, send, window = run(
        rows_finish,
        Y_BACK,
        [(384, 256, "near"), (512, 128), (64, 128, "near")],
        got,
        *surface_set,
        held=t,
    )
    got = exchange(send)
    (new_rows,) = run(
        rows_output, ("near_back",), [(16, NS)], parts, *surface_set, held=t
    )
    (send,) = run(
        columns_slope,
        (),
        [(768, 128)],
        got,
        window,
        jnp.asarray(tables()["slope"]),
        scalars=slab,
        held=t,
        scratch=[pltpu.VMEM((1024, 128), F32)],
    )
    got = exchange(send, "gz")
    out = air_finish_call(place, got, moved, wind, below, above, bottom, top)
    return new_rows, out.reshape(tracer.shape)


def solution(mesh):
    return jax.shard_map(
        shards,
        mesh=mesh,
        in_specs=(P(BOTH, None), P(BOTH, None), P("gx", "gz", None), P("gx", "gz", None)),
        out_specs=(P(BOTH, None), P("gx", "gz", None)),
        check_vma=False,
    )
```

```python
import functools

import jax
import jax.numpy as jnp
import ml_dtypes
import numpy as np
from jax import lax
from jax.experimental import pallas as pl
from jax.experimental.pallas import tpu as pltpu
from jax.sharding import PartitionSpec as P

NS = 2048
DT_WAVE = 0.05
COLUMN_DEPTH = 32.0
DT_AIR = 0.1
NU_AIR = 0.2
TWO_PI = 6.283185307179586
WAVE_UNIT = TWO_PI / NS
BOTH = ("gx", "gz")
F32 = jnp.float32
BF16 = jnp.bfloat16


def halves(matrix):
    exact = np.asarray(matrix, np.float64)
    lead = exact.astype(np.float32).astype(ml_dtypes.bfloat16)
    rest = (exact - lead.astype(np.float64)).astype(np.float32).astype(ml_dtypes.bfloat16)
    return np.stack([lead, rest])


@functools.cache
def tables():
    n128, n16 = np.arange(128), np.arange(16)
    eye16, eye8 = np.eye(16), np.eye(8)
    turn = 2 * np.pi * (np.outer(n128, n128) % 128) / 128
    c, s = np.cos(turn), np.sin(turn)
    wheel = np.concatenate([c, s], 0)
    edge = np.zeros((2, 128, 2, 128))
    edge_back = np.zeros((2, 128, 2, 128))
    sign = (-1.0) ** n128
    for d in range(128):
        if d < 64:
            angle, part = 2 * np.pi * n128 * d / 128, 0
        else:
            angle, part = 2 * np.pi * n128 * (2 * (d - 64) + 1) / 256, 1
        edge[0, d, part] = np.cos(angle)
        edge[1, d, part] = -np.sin(angle) if d else sign
        weight = 2.0 if d else 1.0
        edge_back[part, :, 0, d] = weight * np.cos(angle)
        edge_back[part, :, 1, d] = -weight * np.sin(angle) if d else sign
    edge = edge.reshape(256, 256)
    edge_back = edge_back.reshape(256, 256)
    k8 = np.arange(8)
    angle = 2 * np.pi * np.outer(n16, k8) / 16
    near_re, near_im = np.cos(angle), -np.sin(angle)
    near_im[:, 0] = (-1.0) ** n16
    weight = np.where(k8 == 0, 1.0, 2.0)
    near = np.zeros((16, 16, 2, 8, 16))
    near_back = np.zeros((2, 8, 16, 16, 16))
    for part, table in enumerate((near_re, near_im)):
        near[:, :, part] = table[:, None, :, None] * eye16[None, :, None, :]
        near_back[part] = (table * weight).T[:, None, :, None] * eye16[None, :, None, :]
    near = near.reshape(256, 256)
    near_back = near_back.reshape(256, 256)
    angle = 2 * np.pi * np.outer(n16, n16) / 16
    cx, sx = np.kron(eye8, np.cos(angle)), np.kron(eye8, np.sin(angle))
    comb = np.concatenate([cx, sx], 0)
    y_angle = 2 * np.pi * np.repeat(np.outer(n128, k8), 16, axis=1) / NS
    x_angle = 2 * np.pi * np.tile(np.outer(n128, n16), (1, 8)) / NS
    twist = lambda a: np.stack([np.cos(a), -np.sin(a)]).astype(np.float32)
    r = n128[None, :, None, None]
    x = 16 * n128[None, None, :, None] + n16.reshape(4, 1, 1, 4)
    n = r - x
    with np.errstate(divide="ignore", invalid="ignore"):
        slope = np.where(n % NS == 0, 0.0, (np.pi / NS) * (-1.0) ** (n % 2) / np.tan(np.pi * n / NS))
    slope = slope.reshape(512, 512)
    return dict(
        wheel=halves(wheel),
        edge=halves(edge),
        edge_back=halves(edge_back),
        near=halves(near),
        near_back=halves(near_back),
        comb=halves(comb),
        twist_y=twist(y_angle),
        twist_x=twist(x_angle),
        slope=halves(slope),
    )


def dot(a, b):
    return jnp.dot(a, b, preferred_element_type=F32)


def split(x):
    lead = x.astype(BF16)
    return lead, (x - lead.astype(F32)).astype(BF16)


def from_left(table, x):
    lead, rest = split(x)
    width = x.shape[1]
    both = dot(table[0], jnp.concatenate([lead, rest], 1))
    return both[:, :width] + both[:, width:] + dot(table[1], lead)


def from_right(x, table):
    lead, rest = split(x)
    rows = x.shape[0]
    both = dot(jnp.concatenate([lead, rest], 0), table[0])
    return both[:rows] + both[rows:] + dot(lead, table[1])


def turning(table, sign):
    blocks = []
    for half in (table[0], table[1]):
        c, s = half[:128], half[128:]
        upper, lower = (s, -s) if sign > 0 else (-s, s)
        rows = [jnp.concatenate([c, upper], 1), jnp.concatenate([lower, c], 1)]
        blocks.append(jnp.concatenate(rows, 0))
    return blocks


def slot_zero(shape):
    return lax.broadcasted_iota(jnp.int32, shape, 1) % 128 < 16


def y_twisted(t, parts):
    re, im = parts[:, :128], parts[:, 128:]
    c, s = t["twist_y"][0], t["twist_y"][1]
    return jnp.concatenate([re * c - im * s, re * s + im * c], 0)


def y_joined(t, parts, usual):
    first = from_left(t["edge"], parts)
    out = jnp.where(slot_zero(usual.shape), first, usual)
    return out[:128], out[128:]


def y_forward(t, field):
    parts = y_twisted(t, from_right(field, t["near"]))
    return y_joined(t, parts, from_left(turning(t["wheel"], 1), parts))


def y_back_far(t, re, im):
    parts = jnp.concatenate([re, im], 0)
    usual = from_left(turning(t["wheel"], -1), parts)
    first = from_left(t["edge_back"], parts)
    parts = jnp.where(slot_zero(usual.shape), first, usual)
    c, s = t["twist_y"][0], t["twist_y"][1]
    out = []
    for at in range(0, parts.shape[1], 128):
        re, im = parts[:128, at : at + 128], parts[128:, at : at + 128]
        out.append(jnp.concatenate([re * c + im * s, im * c - re * s], 1))
    return out


def y_back(t, re, im):
    return from_right(y_back_far(t, re, im)[0], t["near_back"])


def x_forward(t, re, im, mirrored):
    parts = jnp.concatenate([re, im], 0)
    if mirrored:
        parts = jnp.concatenate([parts, jnp.concatenate([re, -im], 0)], 1)
    parts = from_left(turning(t["wheel"], 1), parts)
    c, s = t["twist_x"][0], t["twist_x"][1]
    rows = []
    for at in range(0, parts.shape[1], 128):
        re, im = parts[:128, at : at + 128], parts[128:, at : at + 128]
        rows.append(jnp.concatenate([re * c - im * s, re * s + im * c], 1))
    parts = from_right(jnp.concatenate(rows, 0) if mirrored else rows[0], turning(t["comb"], -1))
    out = parts[:128, :128], parts[:128, 128:]
    if mirrored:
        out += parts[128:, :128], parts[128:, 128:]
    return out


def x_back(t, re, im):
    parts = from_right(jnp.concatenate([re, im], 1), turning(t["comb"], 1))
    re, im = parts[:, :128], parts[:, 128:]
    c, s = t["twist_x"][0], t["twist_x"][1]
    parts = jnp.concatenate([re * c + im * s, im * c - re * s], 0)
    out = from_left(turning(t["wheel"], -1), parts)
    return out[:128], out[128:]


def x_waves():
    q1 = lax.broadcasted_iota(jnp.int32, (128, 128), 0)
    lane = lax.broadcasted_iota(jnp.int32, (128, 128), 1)
    kx = q1 + 128 * (lane % 16)
    return jnp.where(kx < NS // 2, kx, kx - NS)


def odd_x():
    kx = x_waves()
    return jnp.where(kx == -(NS // 2), 0, kx).astype(F32) * WAVE_UNIT


def squared_waves(device):
    slot = lax.broadcasted_iota(jnp.int32, (128, 128), 1) // 16
    first = jnp.where(device < 64, 16 * device, 8 + 16 * (device - 64))
    ky = jnp.where(slot == 0, first, slot + 16 * device)
    other = jnp.where((slot == 0) & (device == 0), NS // 2, ky)
    fold = lambda k: jnp.where(k > NS // 2, NS - k, k).astype(F32) * WAVE_UNIT
    wave_x = x_waves().astype(F32) * WAVE_UNIT
    return wave_x * wave_x + fold(ky) * fold(ky), wave_x * wave_x + fold(other) * fold(other)


def even_filter(spectrum, on_re, on_im):
    re, im, mirror_re, mirror_im = spectrum
    plus = (on_re + on_im) * (0.5 / (NS * NS))
    minus = (on_re - on_im) * (0.5 / (NS * NS))
    return re * plus + mirror_re * minus, im * plus + mirror_im * minus


def power_filter(spectrum, squares, power):
    factors = []
    for square in squares:
        magnitude = jnp.sqrt(square)
        factors.append({1: magnitude, 2: square, 3: square * magnitude}[power])
    return even_filter(spectrum, *factors)


def x_derivative(re, im, scale):
    factor = odd_x() * scale
    return -factor * im, factor * re


def y_derivative(re, im):
    d = lax.broadcasted_iota(jnp.int32, (128, 128), 0)
    slot = lax.broadcasted_iota(jnp.int32, (128, 128), 1) // 16
    first = jnp.where(d < 64, 16 * d, 8 + 16 * (d - 64))
    ky = jnp.where(slot == 0, first, slot + 16 * d)
    factor = jnp.where(ky < NS // 2, ky, ky - NS).astype(F32) * (WAVE_UNIT / NS)
    return -factor * im, factor * re


def to_lanes(rows):
    return jnp.concatenate([rows[:, 128 * a : 128 * a + 128] for a in range(16)], 0).T


def pick(ref, fields, index):
    step = 2 * fields
    return ref[pl.ds(2 * index, 128, step), :], ref[pl.ds(2 * index + 1, 128, step), :]


def put(ref, fields, index, values):
    step = 2 * fields
    ref[pl.ds(2 * index, 128, step), :] = values[0]
    ref[pl.ds(2 * index + 1, 128, step), :] = values[1]


def near_core(array):
    return pltpu.with_memory_space_constraint(array, pltpu.VMEM)


def far_away(array):
    return pltpu.with_memory_space_constraint(array, pltpu.HBM)


def run(body, names, outs, *arrays, held, scalars=None, scratch=(), far=()):
    consts = [near_core(held[name]) for name in names]
    lead = [] if scalars is None else [scalars]
    arrays = [far_away(a) if i in far else near_core(a) for i, a in enumerate(arrays)]

    def kernel(*refs):
        at = len(lead)
        tabs = dict(zip(names, refs[at : at + len(names)]))
        body(tabs, *refs[:at], *refs[at + len(names) :])

    vmem = pl.BlockSpec(memory_space=pltpu.VMEM)
    smem = pl.BlockSpec(memory_space=pltpu.SMEM)
    place = lambda out: (pltpu.VMEM if out[-1] == "near" else pltpu.HBM)(out[:2], F32)
    return pl.pallas_call(
        kernel,
        out_shape=[place(out) for out in outs],
        in_specs=[smem] * len(lead) + [vmem] * (len(consts) + len(arrays)),
        out_specs=[vmem] * len(outs),
        scratch_shapes=list(scratch),
        compiler_params=pltpu.CompilerParams(vmem_limit_bytes=16 << 20),
    )(*lead, *consts, *arrays)


Y_FWD = ("near", "wheel", "edge", "twist_y")
Y_BACK = ("near_back", "wheel", "edge_back", "twist_y")
Y_BOTH = ("near", "wheel", "edge", "twist_y", "near_back", "edge_back")
X_BOTH = ("wheel", "comb", "twist_x")
PLANES = (256, 128)
FIELD = (128, 256, "near")
NAMES = ("wheel", "comb", "twist_x", "near", "near_back", "edge", "edge_back", "twist_y")


def start_rows(potential):
    names = ("near", "twist_y", "wheel", "edge")
    sources = [potential] + [jnp.asarray(tables()[name]) for name in names]
    count = len(sources)

    def rows_start(*refs):
        inputs, send, held, sems = refs[:count], refs[count], refs[count + 1 : -1], refs[-1]
        copies = [pltpu.make_async_copy(inputs[i], held[i], sems.at[i]) for i in range(count)]
        for copy in copies:
            copy.start()
        t = dict(zip(names, held[1:]))
        copies[0].wait()
        field = to_lanes(held[0][...])
        copies[1].wait()
        parts = from_right(field, t["near"])
        copies[2].wait()
        parts = y_twisted(t, parts)
        copies[3].wait()
        usual = from_left(turning(t["wheel"], 1), parts)
        copies[4].wait()
        put(send, 1, 0, y_joined(t, parts, usual))

    return pl.pallas_call(
        rows_start,
        out_shape=pltpu.HBM(PLANES, F32),
        in_specs=[pl.BlockSpec(memory_space=pltpu.HBM)] * count,
        out_specs=pl.BlockSpec(memory_space=pltpu.VMEM),
        scratch_shapes=[pltpu.VMEM(c.shape, c.dtype) for c in sources]
        + [pltpu.SemaphoreType.DMA((count,))],
        compiler_params=pltpu.CompilerParams(vmem_limit_bytes=16 << 20),
        name="rows_start",
    )(*[far_away(source) for source in sources])


def hold_tables():
    consts = [jnp.asarray(tables()[name]) for name in NAMES]
    count = len(consts)

    def hold(*refs):
        sems = refs[-1]
        copies = [
            pltpu.make_async_copy(refs[i], refs[count + i], sems.at[i]) for i in range(count)
        ]
        for copy in copies:
            copy.start()
        for copy in copies:
            copy.wait()

    out = pl.pallas_call(
        hold,
        out_shape=[pltpu.VMEM(c.shape, c.dtype) for c in consts],
        in_specs=[pl.BlockSpec(memory_space=pltpu.HBM)] * count,
        out_specs=[pl.BlockSpec(memory_space=pltpu.VMEM)] * count,
        scratch_shapes=[pltpu.SemaphoreType.DMA((count,))],
        compiler_params=pltpu.CompilerParams(vmem_limit_bytes=16 << 20),
        name="hold_tables",
    )(*[far_away(c) for c in consts])
    return dict(zip(NAMES, out))


def stacked(ref):
    return [ref[128 * i : 128 * i + 128, :] for i in range(ref.shape[0] // 128)]


def rows_surface(t, eta, send, lanes, again, window):
    lanes[...] = to_lanes(eta[...])
    window[0:16, :], window[16:32, :] = eta[:, 0:128], eta[:, 128:256]
    spectrum = y_forward(t, lanes[...])
    put(send, 1, 0, spectrum)
    again[0:128, :], again[128:256, :] = spectrum


def rows_along(t, start, surface, along):
    slope = y_back(t, *y_derivative(surface[0:128, :], surface[128:256, :]))
    along[0:128, :] = 1.0 + slope * slope
    along[128:256, :] = slope * y_back(t, *y_derivative(*pick(start, 1, 0)))


def columns_first(t, device, got, send, held):
    spectrum = x_forward(t, *pick(got, 1, 0), True)
    for i, part in enumerate(spectrum):
        held[128 * i : 128 * i + 128, :] = part
    put(send, 1, 0, x_back(t, *power_filter(spectrum, squared_waves(device[0]), 1)))


def columns_first_late(t, device, held, late):
    spectrum = stacked(held)
    squares = squared_waves(device[0])
    put(late, 3, 0, x_back(t, *power_filter(spectrum, squares, 2)))
    put(late, 3, 1, x_back(t, *power_filter(spectrum, squares, 3)))
    put(late, 3, 2, x_back(t, *x_derivative(spectrum[0], spectrum[1], 1.0 / (NS * NS))))


def rows_second(t, got, lanes, surface, send, once):
    once[...] = y_back(t, *pick(got, 1, 0))
    put(send, 2, 0, y_forward(t, -lanes[...] * once[...]))
    put(send, 2, 1, pick(surface, 1, 0))


def columns_second(t, device, got, late, send, held):
    spectrum = x_forward(t, *pick(got, 2, 0), True)
    for i, part in enumerate(spectrum):
        held[128 * i : 128 * i + 128, :] = part
    for i, part in enumerate(pick(got, 2, 1)):
        held[512 + 128 * i : 640 + 128 * i, :] = part
    put(send, 4, 0, x_back(t, *power_filter(spectrum, squared_waves(device[0]), 1)))
    for index in range(3):
        put(send, 4, 1 + index, pick(late, 3, index))


def columns_second_late(t, device, held, late):
    parts = stacked(held)
    put(late, 2, 0, x_back(t, *power_filter(parts[:4], squared_waves(device[0]), 2)))
    re, im = x_forward(t, parts[4], parts[5], False)
    put(late, 2, 1, x_back(t, *x_derivative(re, im, 1.0 / (NS * NS))))


def rows_third(t, got, lanes, send, once, twice):
    eta = lanes[...]
    once[...] = y_back(t, *pick(got, 4, 0))
    twice[...] = y_back(t, *pick(got, 4, 1))
    third = -eta * once[...] - 0.5 * eta * eta * twice[...]
    put(send, 1, 0, y_forward(t, third))


def rows_third_late(t, got, lanes, first_once, once, twice, ready):
    eta = lanes[...]
    thrice = y_back(t, *pick(got, 4, 2))
    ready[0:128, :] = y_back(t, *pick(got, 4, 3))
    ready[128:256, :] = first_once[...] + eta * twice[...] + 0.5 * eta * eta * thrice + once[...]


def columns_third(t, device, got, late, send):
    spectrum = x_forward(t, *pick(got, 1, 0), True)
    put(send, 3, 0, x_back(t, *power_filter(spectrum, squared_waves(device[0]), 1)))
    for index in range(2):
        put(send, 3, 1 + index, pick(late, 2, index))


def rows_finish(t, got, lanes, ready, along, new_rows, send, window):
    pairs = [pick(got, 3, i) for i in range(3)]
    parts = y_back_far(t, *[jnp.concatenate(pair, 1) for pair in zip(*pairs)])
    back = from_right(jnp.concatenate(parts, 0), t["near_back"])
    third_once, second_twice, slope_x = back[:128], back[128:256], back[256:]
    eta = lanes[...]
    speed, known, factor, cross = [ref[at : at + 128, :] for ref in (ready, along) for at in (0, 128)]
    tendency = -(slope_x * speed + cross) + (factor + slope_x * slope_x) * (
        known + third_once + eta * second_twice
    )
    new = (eta + DT_WAVE * tendency).T
    window[...] = new[:32]
    for a in range(16):
        new_rows[:, 128 * a : 128 * a + 128] = new[16 * a : 16 * a + 16]
    group = lax.broadcasted_iota(jnp.int32, (16, 128), 1) // 32
    blocks = []
    for a in range(2):
        rows = new[16 * a : 16 * a + 16]
        turned = [rows] + [pltpu.roll(rows, 32 * k, 1) for k in range(1, 4)]
        for chunk in range(4):
            block = jnp.zeros((4, 128), F32)
            for g in range(4):
                moved = turned[(g - chunk) % 4]
                block = block + jnp.where(group == g, moved, 0.0)[4 * g : 4 * g + 4]
            blocks.append(block)
    block = jnp.concatenate(blocks, 0)
    for at in range(16):
        send[32 * at : 32 * at + 32, :] = block


def columns_slope(t, slab, got, window, table, send, twofold):
    twofold[0:512, :] = got[...]
    twofold[512:1024, :] = got[...]
    start = pl.multiple_of(slab[0] * 32, 32)
    full = from_left(table, twofold[pl.ds(start, 512), :])
    group = lax.broadcasted_iota(jnp.int32, (128, 128), 1) // 32
    total = jnp.zeros((128, 128), F32)
    for g in range(4):
        total = total + jnp.where(group == g, full[128 * g : 128 * g + 128], 0.0)
    total = total + pltpu.roll(total, 64, 1)
    total = total + pltpu.roll(total, 32, 1)
    slope = total.T[:32]
    for at in range(8):
        send[64 * at : 64 * at + 32, :] = slope
        send[64 * at + 32 : 64 * at + 64, :] = window[...]


LEVELS = 8


def block_rows(block, half, level):
    return pl.ds(pl.multiple_of(128 * block + 64 * half + 8 * level, 8), 8)


def rim_rows(block, half, level):
    return pl.ds(pl.multiple_of(256 * half + 128 * level + 8 * block, 8), 8)


def exchanged(v):
    row = lax.broadcasted_iota(jnp.int32, (8, 128), 0)
    for step in (4, 2, 1):
        keep = (row & step) == 0
        out = list(v)
        for i in range(8):
            if not i & step:
                a, b = v[i], v[i + step]
                out[i] = jnp.where(keep, a, pltpu.roll(b, step, 0))
                out[i + step] = jnp.where(keep, pltpu.roll(a, 8 - step, 0), b)
        v = out
    return v


def air_moved(
    place, tracer, wind, before, after, moved, drift, bottom, top, q_s, w_s, moved_s, drift_s, sems
):
    pitch = 2 * LEVELS
    rows = [pl.ds(512 * part, 512) for part in range(4)]
    copies = [
        (before, q_s.at[pl.ds(0, pitch)]),
        (after, q_s.at[pl.ds(pitch + 2048, pitch)]),
    ]
    for part in range(4):
        copies.append((tracer.at[rows[part]], q_s.at[pl.ds(pitch + 512 * part, 512)]))
        copies.append((wind.at[rows[part]], w_s.at[rows[part]]))
    copies = [pltpu.make_async_copy(*pair, sems.at[i]) for i, pair in enumerate(copies)]
    for copy in copies:
        copy.start()
    for copy in copies[:4]:
        copy.wait()
    lane = lax.broadcasted_iota(jnp.int32, (8, 128), 1)
    first, last = lane == 0, lane == 127
    total = (LEVELS * place[1]).astype(F32)
    lifts = [1.0 - ((place[0] * LEVELS + level).astype(F32) + 0.5) / total for level in range(LEVELS)]
    scales = [lift * (DT_AIR * 0.5 * total) for lift in lifts]

    def step(block, carry):
        moved_x, wind_x = ([], []), ([], [])
        for x in range(8):
            at = pl.multiple_of((block * 8 + x) * pitch, pitch)

            def both(ref, shift):
                return [ref[pl.ds(at + shift * pitch + 8 * half, 8), :] for half in range(2)]

            west, mid, east, w = both(q_s, 0), both(q_s, 1), both(q_s, 2), both(w_s, 0)
            back = [pltpu.roll(q, 127, 1) for q in mid]
            ahead = [pltpu.roll(q, 1, 1) for q in mid]
            north = [jnp.where(last, back[1], back[0]), jnp.where(last, mid[1], back[1])]
            south = [jnp.where(first, mid[0], ahead[0]), jnp.where(first, ahead[0], ahead[1])]
            for half in range(2):
                moved_x[half].append(
                    mid[half]
                    + DT_AIR
                    * (
                        -w[half] * (east[half] - west[half]) * 0.5
                        + NU_AIR
                        * (east[half] + west[half] + north[half] + south[half] - 4.0 * mid[half])
                    )
                )
                wind_x[half].append(w[half])
        for half in range(2):
            by_level = exchanged(moved_x[half])
            for level, q in enumerate(by_level):
                moved_s[block_rows(block, half, level), :] = q
            for k in range(2):
                bottom[rim_rows(block, half, k), :] = by_level[k]
                top[rim_rows(block, half, k), :] = by_level[LEVELS - 2 + k]
            for level, w in enumerate(exchanged(wind_x[half])):
                drift_s[block_rows(block, half, level), :] = w * scales[level]
        return carry

    results = []
    for part in range(4):
        for copy in copies[4 + 2 * part : 6 + 2 * part]:
            copy.wait()
        lax.fori_loop(4 * part, 4 * part + 4, step, 0)
        for i, (source, target) in enumerate(((moved_s, moved), (drift_s, drift))):
            out = pltpu.make_async_copy(
                source.at[rows[part]], target.at[rows[part]], sems.at[10 + 2 * part + i]
            )
            out.start()
            results.append(out)
    for out in results:
        out.wait()


def air_finish(place, got, before, moved, drift, below, above, out, *scratch):
    ratio_s, inverse_s, spread_s, slope_s, out_s, sems = scratch
    group, groups = place[0], place[1]
    total = (LEVELS * groups).astype(F32)
    lowest, highest = group == 0, group == groups - 1

    def lift_of(level):
        return 1.0 - ((group * LEVELS + level).astype(F32) + 0.5) / total

    def remap(lower, mid, upper, shift):
        return mid + (0.5 * shift) * ((upper - lower) + shift * (upper - 2.0 * mid + lower))

    slope_s[...] = jnp.concatenate([got[64 * g : 64 * g + 32, :] for g in range(8)], 0).T
    for g in range(8):
        for a in range(2):
            at = 64 * g + 32 + 16 * a
            from_old = pl.multiple_of(jnp.bitwise_xor(group, g) * 32 + 16 * a, 16)
            rows, lanes = slice(16 * g, 16 * g + 16), slice(128 * a, 128 * a + 128)
            new, old = got[at : at + 16, :], before[pl.ds(from_old, 16), :]
            ratio_s[rows, lanes] = (new - old) / (COLUMN_DEPTH - old) * total
            inverse = 1.0 / (COLUMN_DEPTH - new)
            inverse_s[rows, lanes] = inverse * slope_s[rows, lanes]
            spread_s[rows, lanes] = inverse * inverse * (DT_AIR * NU_AIR * total * total)
    lifts = [lift_of(jnp.int32(level)) for level in range(-1, LEVELS + 1)]

    def step(block, carry):
        rows = pl.ds(pl.multiple_of(8 * block, 8), 8)
        for half in range(2):
            lanes = slice(128 * half, 128 * half + 128)
            m = [moved[block_rows(block, half, level), :] for level in range(LEVELS)]
            low = jnp.where(lowest, m[0], below[rim_rows(block, half, 1), :])
            high = jnp.where(highest, m[-1], above[rim_rows(block, half, 0), :])
            outer = [ref[rim_rows(block, half, k), :] for ref, k in ((below, 0), (above, 1))]
            m = [outer[0], low] + m + [high, outer[1]]
            ratio = ratio_s[rows, lanes]
            r = [
                remap(m[i], m[i + 1], m[i + 2], ratio * lifts[i]) for i in range(LEVELS + 2)
            ]
            r[0] = jnp.where(lowest, r[1], r[0])
            r[-1] = jnp.where(highest, r[-2], r[-1])
            inverse, spread = inverse_s[rows, lanes], spread_s[rows, lanes]
            results = []
            for level in range(LEVELS):
                lower, mid, upper = r[level], r[level + 1], r[level + 2]
                results.append(
                    mid
                    + spread * (upper - 2.0 * mid + lower)
                    + drift[block_rows(block, half, level), :] * inverse * (upper - lower)
                )
            for x, value in enumerate(exchanged(results)):
                at = pl.multiple_of((block * 8 + x) * 16 + 8 * half, 8)
                out_s[pl.ds(at, 8), :] = value
        return carry

    copies = []
    for quarter in range(4):
        lax.fori_loop(4 * quarter, 4 * quarter + 4, step, 0)
        rows = pl.ds(512 * quarter, 512)
        copies.append(pltpu.make_async_copy(out_s.at[rows], out.at[rows], sems.at[quarter]))
        copies[-1].start()
    for copy in copies:
        copy.wait()


def air_moved_call(place, tracer, wind, before, after):
    hbm = pl.BlockSpec(memory_space=pltpu.HBM)
    vmem = pl.BlockSpec(memory_space=pltpu.VMEM)
    return pl.pallas_call(
        air_moved,
        out_shape=[pltpu.HBM((2048, 128), F32)] * 2 + [pltpu.HBM((512, 128), F32)] * 2,
        in_specs=[pl.BlockSpec(memory_space=pltpu.SMEM)] + [hbm] * 4,
        out_specs=[hbm, hbm, vmem, vmem],
        scratch_shapes=[
            pltpu.VMEM((2080, 128), F32),
            pltpu.VMEM((2048, 128), F32),
            pltpu.VMEM((2048, 128), F32),
            pltpu.VMEM((2048, 128), F32),
            pltpu.SemaphoreType.DMA((18,)),
        ],
        compiler_params=pltpu.CompilerParams(vmem_limit_bytes=24 << 20),
        name="air_moved",
    )(place, *[far_away(a) for a in (tracer, wind, before, after)])


def air_finish_call(place, got, old, moved, drift, below, above):
    vmem = pl.BlockSpec(memory_space=pltpu.VMEM)
    near = [near_core(a) for a in (got, old, moved, drift, below, above)]
    return pl.pallas_call(
        air_finish,
        out_shape=pltpu.HBM((2048, 128), F32),
        in_specs=[pl.BlockSpec(memory_space=pltpu.SMEM)] + [vmem] * 6,
        out_specs=pl.BlockSpec(memory_space=pltpu.HBM),
        scratch_shapes=[pltpu.VMEM((128, 256), F32)] * 4
        + [pltpu.VMEM((2048, 128), F32), pltpu.SemaphoreType.DMA((4,))],
        compiler_params=pltpu.CompilerParams(vmem_limit_bytes=16 << 20),
        name="air_finish",
    )(place, *near)


def split_halves(air):
    return air.reshape(128, LEVELS, 2, 128).transpose(0, 2, 1, 3).reshape(2048, 128)


def exchange(buffer, axes=BOTH, fields=1):
    if fields == 3:
        buffer = buffer.reshape(128, 3, 2, 128)
    out = lax.all_to_all(buffer, axes, split_axis=0, concat_axis=0, tiled=True)
    return out.reshape(-1, 128)


def shards(elevation, potential, tracer, wind_speed):
    gx, gz = lax.axis_index("gx"), lax.axis_index("gz")
    groups = lax.axis_size("gz")
    device = (gx * groups + gz).astype(jnp.int32).reshape(1)
    slab = gx.astype(jnp.int32).reshape(1)
    place = jnp.concatenate([gz.astype(jnp.int32).reshape(1), jnp.full((1,), groups, jnp.int32)])
    quantity, wind = split_halves(tracer), split_halves(wind_speed)
    size = lax.axis_size("gx")
    ring = [(i, (i + 1) % size) for i in range(size)]
    rise = [(i, i + 1) for i in range(groups - 1)]
    back = lambda pairs: [(j, i) for i, j in pairs]

    start = start_rows(potential)
    got = exchange(start)
    t = hold_tables()
    surface, lanes, spectrum, old = run(
        rows_surface,
        Y_FWD,
        [(256, 128, "near"), FIELD, PLANES, (32, 128)],
        elevation,
        held=t,
        far=(0,),
    )

    send, held = run(
        columns_first, X_BOTH, [(256, 128, "near"), (512, 128, "near")], got, scalars=device, held=t
    )
    got = exchange(send)
    (late,) = run(columns_first_late, X_BOTH, [(768, 128, "near")], held, scalars=device, held=t)
    before = lax.ppermute(quantity[-16:], "gx", ring)
    after = lax.ppermute(quantity[:16], "gx", back(ring))

    for step in range(3):
        pairs = [(i, i ^ (1 << step)) for i in range(groups)]
        old = jnp.concatenate([old, lax.ppermute(old, "gz", pairs)], 0)

    send, first_once = run(rows_second, Y_BOTH, [(512, 128), FIELD], got, lanes, surface, held=t)
    got = exchange(send)
    moved, drift, bottom, top = air_moved_call(place, quantity, wind, before, after)

    send, held = run(
        columns_second,
        X_BOTH,
        [(1024, 128), (768, 128, "near")],
        got,
        late,
        scalars=device,
        held=t,
    )
    got = exchange(send)
    (late,) = run(columns_second_late, X_BOTH, [(512, 128, "near")], held, scalars=device, held=t)
    below = lax.ppermute(top, "gz", rise)
    above = lax.ppermute(bottom, "gz", back(rise))

    send, once, twice = run(rows_third, Y_BOTH, [PLANES, FIELD, FIELD], got, lanes, held=t)
    got_rows, got = got, exchange(send)
    (ready,) = run(
        rows_third_late,
        Y_BACK,
        [(256, 256, "near")],
        got_rows,
        lanes,
        first_once,
        once,
        twice,
        held=t,
    )

    (along,) = run(rows_along, Y_BACK, [(256, 256, "near")], start, spectrum, held=t, far=(0, 1))

    (send,) = run(columns_third, X_BOTH, [(768, 128)], got, late, scalars=device, held=t)
    got = exchange(send, fields=3)

    new_rows, send, window = run(
        rows_finish,
        Y_BACK,
        [(16, NS, "near"), (512, 128, "near"), (32, 128, "near")],
        got,
        lanes,
        ready,
        along,
        held=t,
    )
    got = exchange(send)
    (send,) = run(
        columns_slope,
        (),
        [(512, 128, "near")],
        got,
        window,
        jnp.asarray(tables()["slope"]),
        scalars=slab,
        held=t,
        scratch=[pltpu.VMEM((1024, 128), F32)],
    )
    got = exchange(send, "gz")
    out = air_finish_call(place, got, old, moved, drift, below, above)
    out = out.reshape(128, 2, LEVELS, 128).transpose(0, 2, 1, 3).reshape(tracer.shape)
    return new_rows, out


def solution(mesh):
    return jax.shard_map(
        shards,
        mesh=mesh,
        in_specs=(P(BOTH, None), P(BOTH, None), P("gx", "gz", None), P("gx", "gz", None)),
        out_specs=(P(BOTH, None), P("gx", "gz", None)),
        check_vma=False,
    )
```

```python
import functools

import jax
import jax.numpy as jnp
import ml_dtypes
import numpy as np
from jax import lax
from jax.experimental import pallas as pl
from jax.experimental.pallas import tpu as pltpu
from jax.sharding import PartitionSpec as P

NS = 2048
DT_WAVE = 0.05
COLUMN_DEPTH = 32.0
DT_AIR = 0.1
NU_AIR = 0.2
TWO_PI = 6.283185307179586
WAVE_UNIT = TWO_PI / NS
BOTH = ("gx", "gz")
F32 = jnp.float32
BF16 = jnp.bfloat16


def halves(matrix):
    exact = np.asarray(matrix, np.float64)
    lead = exact.astype(np.float32).astype(ml_dtypes.bfloat16)
    rest = (exact - lead.astype(np.float64)).astype(np.float32).astype(ml_dtypes.bfloat16)
    return np.stack([lead, rest])


@functools.cache
def tables():
    n128, n16 = np.arange(128), np.arange(16)
    eye16, eye8 = np.eye(16), np.eye(8)
    turn = 2 * np.pi * (np.outer(n128, n128) % 128) / 128
    c, s = np.cos(turn), np.sin(turn)
    wheel = np.concatenate([c, s], 0)
    edge = np.zeros((2, 128, 2, 128))
    edge_back = np.zeros((2, 128, 2, 128))
    sign = (-1.0) ** n128
    for d in range(128):
        if d < 64:
            angle, part = 2 * np.pi * n128 * d / 128, 0
        else:
            angle, part = 2 * np.pi * n128 * (2 * (d - 64) + 1) / 256, 1
        edge[0, d, part] = np.cos(angle)
        edge[1, d, part] = -np.sin(angle) if d else sign
        weight = 2.0 if d else 1.0
        edge_back[part, :, 0, d] = weight * np.cos(angle)
        edge_back[part, :, 1, d] = -weight * np.sin(angle) if d else sign
    edge = edge.reshape(256, 256)
    edge_back = edge_back.reshape(256, 256)
    k8 = np.arange(8)
    angle = 2 * np.pi * np.outer(n16, k8) / 16
    near_re, near_im = np.cos(angle), -np.sin(angle)
    near_im[:, 0] = (-1.0) ** n16
    weight = np.where(k8 == 0, 1.0, 2.0)
    near = np.zeros((16, 16, 2, 8, 16))
    near_back = np.zeros((2, 8, 16, 16, 16))
    for part, table in enumerate((near_re, near_im)):
        near[:, :, part] = table[:, None, :, None] * eye16[None, :, None, :]
        near_back[part] = (table * weight).T[:, None, :, None] * eye16[None, :, None, :]
    near = near.reshape(256, 256)
    near_back = near_back.reshape(256, 256)
    angle = 2 * np.pi * np.outer(n16, n16) / 16
    cx, sx = np.kron(eye8, np.cos(angle)), np.kron(eye8, np.sin(angle))
    comb = np.concatenate([cx, sx], 0)
    y_angle = 2 * np.pi * np.repeat(np.outer(n128, k8), 16, axis=1) / NS
    x_angle = 2 * np.pi * np.tile(np.outer(n128, n16), (1, 8)) / NS
    twist = lambda a: np.stack([np.cos(a), -np.sin(a)]).astype(np.float32)
    r = n128[None, :, None, None]
    x = 16 * n128[None, None, :, None] + n16.reshape(4, 1, 1, 4)
    n = r - x
    with np.errstate(divide="ignore", invalid="ignore"):
        slope = np.where(n % NS == 0, 0.0, (np.pi / NS) * (-1.0) ** (n % 2) / np.tan(np.pi * n / NS))
    slope = slope.reshape(512, 512)
    return dict(
        wheel=halves(wheel),
        edge=halves(edge),
        edge_back=halves(edge_back),
        near=halves(near),
        near_back=halves(near_back),
        comb=halves(comb),
        twist_y=twist(y_angle),
        twist_x=twist(x_angle),
        slope=halves(slope),
    )


def dot(a, b):
    return jnp.dot(a, b, preferred_element_type=F32)


def split(x):
    lead = x.astype(BF16)
    return lead, (x - lead.astype(F32)).astype(BF16)


def from_left(table, x):
    lead, rest = split(x)
    width = x.shape[1]
    both = dot(table[0], jnp.concatenate([lead, rest], 1))
    return both[:, :width] + both[:, width:] + dot(table[1], lead)


def from_right(x, table):
    lead, rest = split(x)
    rows = x.shape[0]
    both = dot(jnp.concatenate([lead, rest], 0), table[0])
    return both[:rows] + both[rows:] + dot(lead, table[1])


def turning(table, sign):
    blocks = []
    for half in (table[0], table[1]):
        c, s = half[:128], half[128:]
        upper, lower = (s, -s) if sign > 0 else (-s, s)
        rows = [jnp.concatenate([c, upper], 1), jnp.concatenate([lower, c], 1)]
        blocks.append(jnp.concatenate(rows, 0))
    return blocks


def slot_zero(shape):
    return lax.broadcasted_iota(jnp.int32, shape, 1) % 128 < 16


def y_twisted(t, parts):
    re, im = parts[:, :128], parts[:, 128:]
    c, s = t["twist_y"][0], t["twist_y"][1]
    return jnp.concatenate([re * c - im * s, re * s + im * c], 0)


def y_joined(t, parts, usual):
    first = from_left(t["edge"], parts)
    out = jnp.where(slot_zero(usual.shape), first, usual)
    return out[:128], out[128:]


def y_forward(t, field):
    parts = y_twisted(t, from_right(field, t["near"]))
    return y_joined(t, parts, from_left(turning(t["wheel"], 1), parts))


def y_back_far(t, re, im):
    parts = jnp.concatenate([re, im], 0)
    usual = from_left(turning(t["wheel"], -1), parts)
    first = from_left(t["edge_back"], parts)
    parts = jnp.where(slot_zero(usual.shape), first, usual)
    c, s = t["twist_y"][0], t["twist_y"][1]
    out = []
    for at in range(0, parts.shape[1], 128):
        re, im = parts[:128, at : at + 128], parts[128:, at : at + 128]
        out.append(jnp.concatenate([re * c + im * s, im * c - re * s], 1))
    return out


def y_back(t, re, im):
    return from_right(y_back_far(t, re, im)[0], t["near_back"])


def x_forward(t, re, im, mirrored):
    parts = jnp.concatenate([re, im], 0)
    if mirrored:
        parts = jnp.concatenate([parts, jnp.concatenate([re, -im], 0)], 1)
    parts = from_left(turning(t["wheel"], 1), parts)
    c, s = t["twist_x"][0], t["twist_x"][1]
    rows = []
    for at in range(0, parts.shape[1], 128):
        re, im = parts[:128, at : at + 128], parts[128:, at : at + 128]
        rows.append(jnp.concatenate([re * c - im * s, re * s + im * c], 1))
    parts = from_right(jnp.concatenate(rows, 0) if mirrored else rows[0], turning(t["comb"], -1))
    out = parts[:128, :128], parts[:128, 128:]
    if mirrored:
        out += parts[128:, :128], parts[128:, 128:]
    return out


def x_back(t, re, im):
    parts = from_right(jnp.concatenate([re, im], 1), turning(t["comb"], 1))
    re, im = parts[:, :128], parts[:, 128:]
    c, s = t["twist_x"][0], t["twist_x"][1]
    parts = jnp.concatenate([re * c + im * s, im * c - re * s], 0)
    out = from_left(turning(t["wheel"], -1), parts)
    return out[:128], out[128:]


def x_waves():
    q1 = lax.broadcasted_iota(jnp.int32, (128, 128), 0)
    lane = lax.broadcasted_iota(jnp.int32, (128, 128), 1)
    kx = q1 + 128 * (lane % 16)
    return jnp.where(kx < NS // 2, kx, kx - NS)


def odd_x():
    kx = x_waves()
    return jnp.where(kx == -(NS // 2), 0, kx).astype(F32) * WAVE_UNIT


def squared_waves(device):
    slot = lax.broadcasted_iota(jnp.int32, (128, 128), 1) // 16
    first = jnp.where(device < 64, 16 * device, 8 + 16 * (device - 64))
    ky = jnp.where(slot == 0, first, slot + 16 * device)
    other = jnp.where((slot == 0) & (device == 0), NS // 2, ky)
    fold = lambda k: jnp.where(k > NS // 2, NS - k, k).astype(F32) * WAVE_UNIT
    wave_x = x_waves().astype(F32) * WAVE_UNIT
    return wave_x * wave_x + fold(ky) * fold(ky), wave_x * wave_x + fold(other) * fold(other)


def even_filter(spectrum, on_re, on_im):
    re, im, mirror_re, mirror_im = spectrum
    plus = (on_re + on_im) * (0.5 / (NS * NS))
    minus = (on_re - on_im) * (0.5 / (NS * NS))
    return re * plus + mirror_re * minus, im * plus + mirror_im * minus


def power_filter(spectrum, squares, power):
    factors = []
    for square in squares:
        magnitude = jnp.sqrt(square)
        factors.append({1: magnitude, 2: square, 3: square * magnitude}[power])
    return even_filter(spectrum, *factors)


def x_derivative(re, im, scale):
    factor = odd_x() * scale
    return -factor * im, factor * re


def y_derivative(re, im):
    d = lax.broadcasted_iota(jnp.int32, (128, 128), 0)
    slot = lax.broadcasted_iota(jnp.int32, (128, 128), 1) // 16
    first = jnp.where(d < 64, 16 * d, 8 + 16 * (d - 64))
    ky = jnp.where(slot == 0, first, slot + 16 * d)
    factor = jnp.where(ky < NS // 2, ky, ky - NS).astype(F32) * (WAVE_UNIT / NS)
    return -factor * im, factor * re


def to_lanes(rows):
    return jnp.concatenate([rows[:, 128 * a : 128 * a + 128] for a in range(16)], 0).T


def pick(ref, fields, index):
    step = 2 * fields
    return ref[pl.ds(2 * index, 128, step), :], ref[pl.ds(2 * index + 1, 128, step), :]


def put(ref, fields, index, values):
    step = 2 * fields
    ref[pl.ds(2 * index, 128, step), :] = values[0]
    ref[pl.ds(2 * index + 1, 128, step), :] = values[1]


def near_core(array):
    return pltpu.with_memory_space_constraint(array, pltpu.VMEM)


def far_away(array):
    return pltpu.with_memory_space_constraint(array, pltpu.HBM)


def run(body, names, outs, *arrays, held, scalars=None, scratch=(), far=()):
    consts = [near_core(held[name]) for name in names]
    lead = [] if scalars is None else [scalars]
    arrays = [far_away(a) if i in far else near_core(a) for i, a in enumerate(arrays)]

    def kernel(*refs):
        at = len(lead)
        tabs = dict(zip(names, refs[at : at + len(names)]))
        body(tabs, *refs[:at], *refs[at + len(names) :])

    vmem = pl.BlockSpec(memory_space=pltpu.VMEM)
    smem = pl.BlockSpec(memory_space=pltpu.SMEM)
    place = lambda out: (pltpu.VMEM if out[-1] == "near" else pltpu.HBM)(out[:2], F32)
    return pl.pallas_call(
        kernel,
        out_shape=[place(out) for out in outs],
        in_specs=[smem] * len(lead) + [vmem] * (len(consts) + len(arrays)),
        out_specs=[vmem] * len(outs),
        scratch_shapes=list(scratch),
        compiler_params=pltpu.CompilerParams(vmem_limit_bytes=16 << 20),
    )(*lead, *consts, *arrays)


Y_FWD = ("near", "wheel", "edge", "twist_y")
Y_BACK = ("near_back", "wheel", "edge_back", "twist_y")
Y_BOTH = ("near", "wheel", "edge", "twist_y", "near_back", "edge_back")
X_BOTH = ("wheel", "comb", "twist_x")
PLANES = (256, 128)
FIELD = (128, 256, "near")
NAMES = ("wheel", "comb", "twist_x", "near", "near_back", "edge", "edge_back", "twist_y")


def start_rows(potential):
    names = ("near", "twist_y", "wheel", "edge")
    sources = [potential] + [jnp.asarray(tables()[name]) for name in names]
    count = len(sources)

    def rows_start(*refs):
        inputs, send, held, sems = refs[:count], refs[count], refs[count + 1 : -1], refs[-1]
        copies = [pltpu.make_async_copy(inputs[i], held[i], sems.at[i]) for i in range(count)]
        for copy in copies:
            copy.start()
        t = dict(zip(names, held[1:]))
        copies[0].wait()
        field = to_lanes(held[0][...])
        copies[1].wait()
        parts = from_right(field, t["near"])
        copies[2].wait()
        parts = y_twisted(t, parts)
        copies[3].wait()
        usual = from_left(turning(t["wheel"], 1), parts)
        copies[4].wait()
        put(send, 1, 0, y_joined(t, parts, usual))

    return pl.pallas_call(
        rows_start,
        out_shape=pltpu.HBM(PLANES, F32),
        in_specs=[pl.BlockSpec(memory_space=pltpu.HBM)] * count,
        out_specs=pl.BlockSpec(memory_space=pltpu.VMEM),
        scratch_shapes=[pltpu.VMEM(c.shape, c.dtype) for c in sources]
        + [pltpu.SemaphoreType.DMA((count,))],
        compiler_params=pltpu.CompilerParams(vmem_limit_bytes=16 << 20),
        name="rows_start",
    )(*[far_away(source) for source in sources])


def hold_tables():
    consts = [jnp.asarray(tables()[name]) for name in NAMES]
    count = len(consts)

    def hold(*refs):
        sems = refs[-1]
        copies = [
            pltpu.make_async_copy(refs[i], refs[count + i], sems.at[i]) for i in range(count)
        ]
        for copy in copies:
            copy.start()
        for copy in copies:
            copy.wait()

    out = pl.pallas_call(
        hold,
        out_shape=[pltpu.VMEM(c.shape, c.dtype) for c in consts],
        in_specs=[pl.BlockSpec(memory_space=pltpu.HBM)] * count,
        out_specs=[pl.BlockSpec(memory_space=pltpu.VMEM)] * count,
        scratch_shapes=[pltpu.SemaphoreType.DMA((count,))],
        compiler_params=pltpu.CompilerParams(vmem_limit_bytes=16 << 20),
        name="hold_tables",
    )(*[far_away(c) for c in consts])
    return dict(zip(NAMES, out))


def stacked(ref):
    return [ref[128 * i : 128 * i + 128, :] for i in range(ref.shape[0] // 128)]


def rows_surface(t, eta, send, lanes, again, window):
    lanes[...] = to_lanes(eta[...])
    window[0:16, :], window[16:32, :] = eta[:, 0:128], eta[:, 128:256]
    spectrum = y_forward(t, lanes[...])
    put(send, 1, 0, spectrum)
    again[0:128, :], again[128:256, :] = spectrum


def rows_along(t, start, surface, along):
    slope = y_back(t, *y_derivative(surface[0:128, :], surface[128:256, :]))
    along[0:128, :] = 1.0 + slope * slope
    along[128:256, :] = slope * y_back(t, *y_derivative(*pick(start, 1, 0)))


def columns_first(t, device, got, send, held):
    spectrum = x_forward(t, *pick(got, 1, 0), True)
    for i, part in enumerate(spectrum):
        held[128 * i : 128 * i + 128, :] = part
    put(send, 1, 0, x_back(t, *power_filter(spectrum, squared_waves(device[0]), 1)))


def columns_first_late(t, device, held, late):
    spectrum = stacked(held)
    squares = squared_waves(device[0])
    put(late, 3, 0, x_back(t, *power_filter(spectrum, squares, 2)))
    put(late, 3, 1, x_back(t, *power_filter(spectrum, squares, 3)))
    put(late, 3, 2, x_back(t, *x_derivative(spectrum[0], spectrum[1], 1.0 / (NS * NS))))


def rows_second(t, got, lanes, surface, send, once):
    once[...] = y_back(t, *pick(got, 1, 0))
    put(send, 2, 0, y_forward(t, -lanes[...] * once[...]))
    put(send, 2, 1, pick(surface, 1, 0))


def columns_second(t, device, got, late, send, held):
    spectrum = x_forward(t, *pick(got, 2, 0), True)
    for i, part in enumerate(spectrum):
        held[128 * i : 128 * i + 128, :] = part
    for i, part in enumerate(pick(got, 2, 1)):
        held[512 + 128 * i : 640 + 128 * i, :] = part
    put(send, 4, 0, x_back(t, *power_filter(spectrum, squared_waves(device[0]), 1)))
    for index in range(3):
        put(send, 4, 1 + index, pick(late, 3, index))


def columns_second_late(t, device, held, late):
    parts = stacked(held)
    put(late, 2, 0, x_back(t, *power_filter(parts[:4], squared_waves(device[0]), 2)))
    re, im = x_forward(t, parts[4], parts[5], False)
    put(late, 2, 1, x_back(t, *x_derivative(re, im, 1.0 / (NS * NS))))


def rows_third(t, got, lanes, send, once, twice):
    eta = lanes[...]
    once[...] = y_back(t, *pick(got, 4, 0))
    twice[...] = y_back(t, *pick(got, 4, 1))
    third = -eta * once[...] - 0.5 * eta * eta * twice[...]
    put(send, 1, 0, y_forward(t, third))


def rows_third_late(t, got, lanes, first_once, once, twice, ready):
    eta = lanes[...]
    thrice = y_back(t, *pick(got, 4, 2))
    ready[0:128, :] = y_back(t, *pick(got, 4, 3))
    ready[128:256, :] = first_once[...] + eta * twice[...] + 0.5 * eta * eta * thrice + once[...]


def columns_third(t, device, got, late, send):
    spectrum = x_forward(t, *pick(got, 1, 0), True)
    put(send, 3, 0, x_back(t, *power_filter(spectrum, squared_waves(device[0]), 1)))
    for index in range(2):
        put(send, 3, 1 + index, pick(late, 2, index))


def rows_finish(t, got, lanes, ready, along, new_rows, send, window):
    pairs = [pick(got, 3, i) for i in range(3)]
    parts = y_back_far(t, *[jnp.concatenate(pair, 1) for pair in zip(*pairs)])
    back = from_right(jnp.concatenate(parts, 0), t["near_back"])
    third_once, second_twice, slope_x = back[:128], back[128:256], back[256:]
    eta = lanes[...]
    speed, known, factor, cross = [ref[at : at + 128, :] for ref in (ready, along) for at in (0, 128)]
    tendency = -(slope_x * speed + cross) + (factor + slope_x * slope_x) * (
        known + third_once + eta * second_twice
    )
    new = (eta + DT_WAVE * tendency).T
    window[...] = new[:32]
    for a in range(16):
        new_rows[:, 128 * a : 128 * a + 128] = new[16 * a : 16 * a + 16]
    group = lax.broadcasted_iota(jnp.int32, (16, 128), 1) // 32
    blocks = []
    for a in range(2):
        rows = new[16 * a : 16 * a + 16]
        turned = [rows] + [pltpu.roll(rows, 32 * k, 1) for k in range(1, 4)]
        for chunk in range(4):
            block = jnp.zeros((4, 128), F32)
            for g in range(4):
                moved = turned[(g - chunk) % 4]
                block = block + jnp.where(group == g, moved, 0.0)[4 * g : 4 * g + 4]
            blocks.append(block)
    block = jnp.concatenate(blocks, 0)
    for at in range(16):
        send[32 * at : 32 * at + 32, :] = block


def columns_slope(t, slab, got, window, table, send, twofold):
    twofold[0:512, :] = got[...]
    twofold[512:1024, :] = got[...]
    start = pl.multiple_of(slab[0] * 32, 32)
    full = from_left(table, twofold[pl.ds(start, 512), :])
    group = lax.broadcasted_iota(jnp.int32, (128, 128), 1) // 32
    total = jnp.zeros((128, 128), F32)
    for g in range(4):
        total = total + jnp.where(group == g, full[128 * g : 128 * g + 128], 0.0)
    total = total + pltpu.roll(total, 64, 1)
    total = total + pltpu.roll(total, 32, 1)
    slope = total.T[:32]
    for at in range(8):
        send[64 * at : 64 * at + 32, :] = slope
        send[64 * at + 32 : 64 * at + 64, :] = window[...]


LEVELS = 8


def block_rows(block, half, level):
    return pl.ds(pl.multiple_of(128 * block + 64 * half + 8 * level, 8), 8)


def rim_rows(block, half, level):
    return pl.ds(pl.multiple_of(256 * half + 128 * level + 8 * block, 8), 8)


def exchanged(v):
    row = lax.broadcasted_iota(jnp.int32, (8, 128), 0)
    for step in (4, 2, 1):
        keep = (row & step) == 0
        out = list(v)
        for i in range(8):
            if not i & step:
                a, b = v[i], v[i + step]
                out[i] = jnp.where(keep, a, pltpu.roll(b, step, 0))
                out[i + step] = jnp.where(keep, pltpu.roll(a, 8 - step, 0), b)
        v = out
    return v


def air_moved(
    place, tracer, wind, before, after, moved, drift, bottom, top, q_s, w_s, moved_s, drift_s, sems
):
    pitch = 2 * LEVELS
    rows = [pl.ds(512 * part, 512) for part in range(4)]
    copies = [
        (before, q_s.at[pl.ds(0, pitch)]),
        (after, q_s.at[pl.ds(pitch + 2048, pitch)]),
    ]
    for part in range(4):
        copies.append((tracer.at[rows[part]], q_s.at[pl.ds(pitch + 512 * part, 512)]))
        copies.append((wind.at[rows[part]], w_s.at[rows[part]]))
    copies = [pltpu.make_async_copy(*pair, sems.at[i]) for i, pair in enumerate(copies)]
    for copy in copies:
        copy.start()
    for copy in copies[:4]:
        copy.wait()
    lane = lax.broadcasted_iota(jnp.int32, (8, 128), 1)
    first, last = lane == 0, lane == 127
    total = (LEVELS * place[1]).astype(F32)
    lifts = [1.0 - ((place[0] * LEVELS + level).astype(F32) + 0.5) / total for level in range(LEVELS)]
    scales = [lift * (DT_AIR * 0.5 * total) for lift in lifts]

    def step(block, carry):
        moved_x, wind_x = ([], []), ([], [])
        for x in range(8):
            at = pl.multiple_of((block * 8 + x) * pitch, pitch)

            def both(ref, shift):
                return [ref[pl.ds(at + shift * pitch + 8 * half, 8), :] for half in range(2)]

            west, mid, east, w = both(q_s, 0), both(q_s, 1), both(q_s, 2), both(w_s, 0)
            back = [pltpu.roll(q, 127, 1) for q in mid]
            ahead = [pltpu.roll(q, 1, 1) for q in mid]
            north = [jnp.where(last, back[1], back[0]), jnp.where(last, mid[1], back[1])]
            south = [jnp.where(first, mid[0], ahead[0]), jnp.where(first, ahead[0], ahead[1])]
            for half in range(2):
                moved_x[half].append(
                    mid[half]
                    + DT_AIR
                    * (
                        -w[half] * (east[half] - west[half]) * 0.5
                        + NU_AIR
                        * (east[half] + west[half] + north[half] + south[half] - 4.0 * mid[half])
                    )
                )
                wind_x[half].append(w[half])
        for half in range(2):
            by_level = exchanged(moved_x[half])
            for level, q in enumerate(by_level):
                moved_s[block_rows(block, half, level), :] = q
            for k in range(2):
                bottom[rim_rows(block, half, k), :] = by_level[k]
                top[rim_rows(block, half, k), :] = by_level[LEVELS - 2 + k]
            for level, w in enumerate(exchanged(wind_x[half])):
                drift_s[block_rows(block, half, level), :] = w * scales[level]
        return carry

    results = []
    for part in range(4):
        for copy in copies[4 + 2 * part : 6 + 2 * part]:
            copy.wait()
        lax.fori_loop(4 * part, 4 * part + 4, step, 0)
        for i, (source, target) in enumerate(((moved_s, moved), (drift_s, drift))):
            out = pltpu.make_async_copy(
                source.at[rows[part]], target.at[rows[part]], sems.at[10 + 2 * part + i]
            )
            out.start()
            results.append(out)
    for out in results:
        out.wait()


def air_finish(place, got, before, moved, drift, below, above, out, *scratch):
    ratio_s, inverse_s, spread_s, slope_s, out_s, sems = scratch
    group, groups = place[0], place[1]
    total = (LEVELS * groups).astype(F32)
    lowest, highest = group == 0, group == groups - 1

    def lift_of(level):
        return 1.0 - ((group * LEVELS + level).astype(F32) + 0.5) / total

    def remap(lower, mid, upper, shift):
        return mid + (0.5 * shift) * ((upper - lower) + shift * (upper - 2.0 * mid + lower))

    slope_s[...] = jnp.concatenate([got[64 * g : 64 * g + 32, :] for g in range(8)], 0).T
    for g in range(8):
        for a in range(2):
            at = 64 * g + 32 + 16 * a
            from_old = pl.multiple_of(jnp.bitwise_xor(group, g) * 32 + 16 * a, 16)
            rows, lanes = slice(16 * g, 16 * g + 16), slice(128 * a, 128 * a + 128)
            new, old = got[at : at + 16, :], before[pl.ds(from_old, 16), :]
            ratio_s[rows, lanes] = (new - old) / (COLUMN_DEPTH - old) * total
            inverse = 1.0 / (COLUMN_DEPTH - new)
            inverse_s[rows, lanes] = inverse * slope_s[rows, lanes]
            spread_s[rows, lanes] = inverse * inverse * (DT_AIR * NU_AIR * total * total)
    lifts = [lift_of(jnp.int32(level)) for level in range(-1, LEVELS + 1)]

    def step(block, carry):
        rows = pl.ds(pl.multiple_of(8 * block, 8), 8)
        for half in range(2):
            lanes = slice(128 * half, 128 * half + 128)
            m = [moved[block_rows(block, half, level), :] for level in range(LEVELS)]
            low = jnp.where(lowest, m[0], below[rim_rows(block, half, 1), :])
            high = jnp.where(highest, m[-1], above[rim_rows(block, half, 0), :])
            outer = [ref[rim_rows(block, half, k), :] for ref, k in ((below, 0), (above, 1))]
            m = [outer[0], low] + m + [high, outer[1]]
            ratio = ratio_s[rows, lanes]
            r = [
                remap(m[i], m[i + 1], m[i + 2], ratio * lifts[i]) for i in range(LEVELS + 2)
            ]
            r[0] = jnp.where(lowest, r[1], r[0])
            r[-1] = jnp.where(highest, r[-2], r[-1])
            inverse, spread = inverse_s[rows, lanes], spread_s[rows, lanes]
            results = []
            for level in range(LEVELS):
                lower, mid, upper = r[level], r[level + 1], r[level + 2]
                results.append(
                    mid
                    + spread * (upper - 2.0 * mid + lower)
                    + drift[block_rows(block, half, level), :] * inverse * (upper - lower)
                )
            for x, value in enumerate(exchanged(results)):
                at = pl.multiple_of((block * 8 + x) * 16 + 8 * half, 8)
                out_s[pl.ds(at, 8), :] = value
        return carry

    copies = []
    for part in range(8):
        lax.fori_loop(2 * part, 2 * part + 2, step, 0)
        rows = pl.ds(256 * part, 256)
        copies.append(pltpu.make_async_copy(out_s.at[rows], out.at[rows], sems.at[part]))
        copies[-1].start()
    for copy in copies:
        copy.wait()


def air_moved_call(place, tracer, wind, before, after):
    hbm = pl.BlockSpec(memory_space=pltpu.HBM)
    vmem = pl.BlockSpec(memory_space=pltpu.VMEM)
    return pl.pallas_call(
        air_moved,
        out_shape=[pltpu.HBM((2048, 128), F32)] * 2 + [pltpu.HBM((512, 128), F32)] * 2,
        in_specs=[pl.BlockSpec(memory_space=pltpu.SMEM)] + [hbm] * 4,
        out_specs=[hbm, hbm, vmem, vmem],
        scratch_shapes=[
            pltpu.VMEM((2080, 128), F32),
            pltpu.VMEM((2048, 128), F32),
            pltpu.VMEM((2048, 128), F32),
            pltpu.VMEM((2048, 128), F32),
            pltpu.SemaphoreType.DMA((18,)),
        ],
        compiler_params=pltpu.CompilerParams(vmem_limit_bytes=24 << 20),
        name="air_moved",
    )(place, *[far_away(a) for a in (tracer, wind, before, after)])


def air_finish_call(place, got, old, moved, drift, below, above):
    vmem = pl.BlockSpec(memory_space=pltpu.VMEM)
    near = [near_core(a) for a in (got, old, moved, drift, below, above)]
    return pl.pallas_call(
        air_finish,
        out_shape=pltpu.HBM((2048, 128), F32),
        in_specs=[pl.BlockSpec(memory_space=pltpu.SMEM)] + [vmem] * 6,
        out_specs=pl.BlockSpec(memory_space=pltpu.HBM),
        scratch_shapes=[pltpu.VMEM((128, 256), F32)] * 4
        + [pltpu.VMEM((2048, 128), F32), pltpu.SemaphoreType.DMA((8,))],
        compiler_params=pltpu.CompilerParams(vmem_limit_bytes=16 << 20),
        name="air_finish",
    )(place, *near)


def split_halves(air):
    return air.reshape(128, LEVELS, 2, 128).transpose(0, 2, 1, 3).reshape(2048, 128)


def exchange(buffer, axes=BOTH, fields=1):
    if fields == 3:
        buffer = buffer.reshape(128, 3, 2, 128)
    out = lax.all_to_all(buffer, axes, split_axis=0, concat_axis=0, tiled=True)
    return out.reshape(-1, 128)


def shards(elevation, potential, tracer, wind_speed):
    gx, gz = lax.axis_index("gx"), lax.axis_index("gz")
    groups = lax.axis_size("gz")
    device = (gx * groups + gz).astype(jnp.int32).reshape(1)
    slab = gx.astype(jnp.int32).reshape(1)
    place = jnp.concatenate([gz.astype(jnp.int32).reshape(1), jnp.full((1,), groups, jnp.int32)])
    quantity, wind = split_halves(tracer), split_halves(wind_speed)
    size = lax.axis_size("gx")
    ring = [(i, (i + 1) % size) for i in range(size)]
    rise = [(i, i + 1) for i in range(groups - 1)]
    back = lambda pairs: [(j, i) for i, j in pairs]

    start = start_rows(potential)
    got = exchange(start)
    t = hold_tables()
    surface, lanes, spectrum, old = run(
        rows_surface,
        Y_FWD,
        [(256, 128, "near"), FIELD, PLANES, (32, 128)],
        elevation,
        held=t,
        far=(0,),
    )

    send, held = run(
        columns_first, X_BOTH, [(256, 128, "near"), (512, 128, "near")], got, scalars=device, held=t
    )
    got = exchange(send)
    (late,) = run(columns_first_late, X_BOTH, [(768, 128, "near")], held, scalars=device, held=t)
    before = lax.ppermute(quantity[-16:], "gx", ring)
    after = lax.ppermute(quantity[:16], "gx", back(ring))

    for step in range(3):
        pairs = [(i, i ^ (1 << step)) for i in range(groups)]
        old = jnp.concatenate([old, lax.ppermute(old, "gz", pairs)], 0)

    send, first_once = run(rows_second, Y_BOTH, [(512, 128), FIELD], got, lanes, surface, held=t)
    got = exchange(send)
    moved, drift, bottom, top = air_moved_call(place, quantity, wind, before, after)

    send, held = run(
        columns_second,
        X_BOTH,
        [(1024, 128), (768, 128, "near")],
        got,
        late,
        scalars=device,
        held=t,
    )
    got = exchange(send)
    (late,) = run(columns_second_late, X_BOTH, [(512, 128, "near")], held, scalars=device, held=t)
    below = lax.ppermute(top, "gz", rise)
    above = lax.ppermute(bottom, "gz", back(rise))

    send, once, twice = run(rows_third, Y_BOTH, [PLANES, FIELD, FIELD], got, lanes, held=t)
    got_rows, got = got, exchange(send)
    (ready,) = run(
        rows_third_late,
        Y_BACK,
        [(256, 256, "near")],
        got_rows,
        lanes,
        first_once,
        once,
        twice,
        held=t,
    )

    (along,) = run(rows_along, Y_BACK, [(256, 256, "near")], start, spectrum, held=t, far=(0, 1))

    (send,) = run(columns_third, X_BOTH, [(768, 128)], got, late, scalars=device, held=t)
    got = exchange(send, fields=3)

    new_rows, send, window = run(
        rows_finish,
        Y_BACK,
        [(16, NS, "near"), (512, 128, "near"), (32, 128, "near")],
        got,
        lanes,
        ready,
        along,
        held=t,
    )
    got = exchange(send)
    (send,) = run(
        columns_slope,
        (),
        [(512, 128, "near")],
        got,
        window,
        jnp.asarray(tables()["slope"]),
        scalars=slab,
        held=t,
        scratch=[pltpu.VMEM((1024, 128), F32)],
    )
    got = exchange(send, "gz")
    out = air_finish_call(place, got, old, moved, drift, below, above)
    out = out.reshape(128, 2, LEVELS, 128).transpose(0, 2, 1, 3).reshape(tracer.shape)
    return new_rows, out


def solution(mesh):
    return jax.shard_map(
        shards,
        mesh=mesh,
        in_specs=(P(BOTH, None), P(BOTH, None), P("gx", "gz", None), P("gx", "gz", None)),
        out_specs=(P(BOTH, None), P("gx", "gz", None)),
        check_vma=False,
    )
```
